256 devices in a mesh: sel: 64 (over y, z, core), mdl: 4 (over x).
Axes of the slice: x: 4, y: 4, z: 8, core: 2. Of those that a mesh axis runs over, the one named last changes fastest.
Arguments:
- patches: bfloat16 [49152, 1408], P('sel', 'mdl'), may hold values from -6 to 6
- text: bfloat16 [8192, 1024], P('sel', 'mdl'), may hold values from -64 to 64
- ref_proj: bfloat16 [1408, 1024], P(None, 'mdl'), may hold values from -0.15625 to 0.15625
- w_up: bfloat16 [1408, 6144], P(None, 'mdl'), may hold values from -0.15625 to 0.15625
- w_down: bfloat16 [6144, 1408], P('mdl'), may hold values from -0.078125 to 0.078125
- kept_index: int32 [4096], P('sel'), may hold values from 0 to 127, as said below
- dest: int32 [4096], P('sel'), may hold values from 0 to 63, as said below
- cotan: bfloat16 [24576, 1408], P('sel', 'mdl'), may hold values from -16 to 16
Outputs:
- ref_loss: float32 [8192], P('sel')
- learnability: float32 [4096], P('sel')
- grad_up: float32 [1408, 6144], P('sel', 'mdl')
The draws below stay inside these ranges and needn't reach their ends.
Inputs may be any that keep to these rules, and one draw needn't show every extreme that they name: `kept_index`: the 64 entries of one scorer shard are distinct. `dest`: on each scorer shard at most 2 kept entries name the same learner shard; one learner shard is named by exactly 2 kept entries of every scorer shard.
All inputs are finite; a program needn't handle non-finite values.
Results may differ from the reference program's by a relative error of at most 0.019.
Values may be sent and summed in bfloat16 or wider, within the bound.
A program may use at most 128 MiB of HBM per device.

```python
import math
import jax
import jax.numpy as jnp
from jax import lax

D = 1408
FF = 6144
EMB = 1024
P_SIZE = 6
EX_DEV = 128
K_DEV = 64
EX = 8192
KEPT = 4096


def draw_text(key, part):
    key_base, key_scale = jax.random.split(key, 2)
    base_vals = jnp.clip(jax.random.normal(key_base, (EX, EMB), jnp.float32), -6.0, 6.0)
    row_scale = jnp.exp(jax.random.uniform(key_scale, (EX, 1), jnp.float32, 0.0, math.log(10.0)))
    return jnp.clip(base_vals * row_scale, -64.0, 64.0).astype(jnp.bfloat16)


def pick_rows(group_key):
    return jax.random.permutation(group_key, EX_DEV)[:K_DEV]


def draw_kept_index(key, part):
    n_groups = EX // EX_DEV
    group_keys = jax.random.split(key, n_groups)
    return jax.vmap(pick_rows)(group_keys).reshape(KEPT).astype(jnp.int32)


def draw_dest(key, part):
    n_groups = KEPT // K_DEV
    key_shift, key_source, key_place, key_label = jax.random.split(key, 4)
    half_count = n_groups // 2
    shifts = jax.random.randint(key_shift, (half_count,), 0, K_DEV + 1).astype(jnp.int32)
    shifts = shifts.at[0].set(K_DEV)
    dest_loads = jnp.stack([K_DEV + shifts, K_DEV - shifts], axis=1).reshape(n_groups)
    bounds = jnp.cumsum(dest_loads).astype(jnp.int32)
    slot_ids = jnp.arange(KEPT, dtype=jnp.int32)
    sorted_dest = jnp.sum((bounds[None, :] <= slot_ids[:, None]).astype(jnp.int32), axis=1)
    slot_table = sorted_dest.reshape(K_DEV, n_groups).T
    source_order = jax.random.permutation(key_source, n_groups)
    slot_table = slot_table[source_order]
    slot_table = jax.random.permutation(key_place, slot_table, axis=1, independent=True)
    relabel = jax.random.permutation(key_label, n_groups).astype(jnp.int32)
    return relabel[slot_table].reshape(KEPT).astype(jnp.int32)


def with_spikes(result, rng, source, target, parts, factor):
    def block_of(position):
        return (jnp.arange(result.shape[position]) // (result.shape[position] // parts)).reshape((-1,) + (1,) * (result.ndim - 1 - position))

    near = jax.random.permutation(rng, parts)[block_of(target)]
    second = (block_of(target) + parts // 2) % parts
    return jnp.where((block_of(source) == near) | (block_of(source) == second), factor * result, result)


def levels(rng, shape, pieces, smallest, high):
    factor_of, own = 1.0, jax.random.fold_in(rng, 6)
    for dim, parts in pieces:
        draws = jnp.exp(jax.random.uniform(jax.random.fold_in(own, dim), (parts,), jnp.float32, smallest / len(pieces), high / len(pieces)))
        factor_of = factor_of * jnp.repeat(draws, shape[dim] // parts).reshape([-1 if axis == dim else 1 for axis in range(len(shape))])
    return factor_of


def scatter_about(own_key, shape, width, limit, pieces=(), kind=jnp.bfloat16):
    values = width * jax.random.normal(own_key, shape, jnp.float32)
    if pieces:
        values = values * levels(own_key, shape, pieces, -0.22, 0.18)
    return jnp.clip(values, -limit, limit).astype(kind)


def gaussian_with(stream_key, dims, deviation, most, pieces, heavy, kind=jnp.bfloat16):
    values = deviation * jax.random.normal(stream_key, dims, jnp.float32)
    if pieces:
        values = values * levels(stream_key, dims, pieces, -0.22, 0.18)
    return jnp.clip(with_spikes(values, jax.random.fold_in(stream_key, 3), *heavy), -most, most).astype(kind)


def setup_inputs(seed: int = 0) -> dict:
    keys = jax.random.split(jax.random.key(seed), 9)
    patches = scatter_about(keys[0], (EX * P_SIZE, D), 1.0, 6.0, ((0, 64), (1, 4)))
    text = draw_text(jax.random.fold_in(keys[8], 71), 0)
    ref_proj = scatter_about(keys[2], (D, EMB), D ** -0.5, 0.15625, ((1, 4),))
    w_up = scatter_about(keys[3], (D, FF), D ** -0.5, 0.15625, ((1, 4),))
    w_down = scatter_about(keys[4], (FF, D), FF ** -0.5, 0.078125, ((0, 4),))
    kept_index = draw_kept_index(jax.random.fold_in(keys[8], 71), 0)
    dest = draw_dest(jax.random.fold_in(keys[8], 71), 0)
    cotan = gaussian_with(keys[7], (KEPT * P_SIZE, D), 1.0, 16.0, ((0, 64), (1, 4)), (0, 1, 64, 4.0))
    return {"patches": patches, "text": text, "ref_proj": ref_proj, "w_up": w_up, "w_down": w_down, "kept_index": kept_index, "dest": dest, "cotan": cotan}


logit_scale = 64.0
eps = 1e-06

def gelu_parts(pre_act):
    cumul = 0.5 * (1.0 + lax.erf(pre_act * 0.7071067811865476))
    density = jnp.exp(-0.5 * pre_act * pre_act) * 0.3989422804014327
    return (pre_act * cumul, cumul + pre_act * density)

def unit_rows(values):
    norm_sq = lax.optimization_barrier(jnp.sum(values * values, axis=1))
    return (values * lax.rsqrt(norm_sq + eps)[:, None]).astype(jnp.bfloat16)

def reference(patches, text, ref_proj, w_up, w_down, kept_index, dest, cotan):
    n_sel = EX // EX_DEV
    blocks = patches.reshape(EX, P_SIZE, D)
    pooled = lax.optimization_barrier(jnp.mean(blocks, axis=1, dtype=jnp.float32)).astype(jnp.bfloat16)
    img_hat = unit_rows(jnp.dot(pooled, ref_proj, preferred_element_type=jnp.float32))
    text_hat = unit_rows(text.astype(jnp.float32))

    def loss_block(args_pair):
        rows_hat, own_cols = args_pair
        scores = logit_scale * jnp.dot(rows_hat, text_hat.T, preferred_element_type=jnp.float32)
        log_total = jnp.log(lax.optimization_barrier(jnp.sum(jnp.exp(scores), axis=1)))
        own_score = jnp.take_along_axis(scores, own_cols[:, None], axis=1)[:, 0]
        return log_total - own_score
    ref_loss = lax.map(loss_block, (img_hat.reshape(n_sel, EX_DEV, EMB), jnp.arange(EX, dtype=jnp.int32).reshape(n_sel, EX_DEV))).reshape(EX)
    kept_global = jnp.arange(KEPT, dtype=jnp.int32) // K_DEV * EX_DEV + kept_index
    dest_counts = lax.optimization_barrier(jnp.sum((dest[:, None] == jnp.arange(n_sel, dtype=jnp.int32)[None, :]).astype(jnp.float32), axis=0))
    row_weight = 1.0 / dest_counts[dest]
    kept_tok = blocks[kept_global].reshape(n_sel, K_DEV, P_SIZE, D)
    kept_cot = cotan.reshape(n_sel, K_DEV, P_SIZE, D)

    def learner_step(total_up, inputs):
        block_tok, block_cot, block_weight = inputs
        tok_rows = block_tok.reshape(K_DEV * P_SIZE, D)
        weighted = (block_cot.astype(jnp.float32) * block_weight[:, None, None]).astype(jnp.bfloat16).reshape(K_DEV * P_SIZE, D)
        pre_act = jnp.dot(tok_rows, w_up, preferred_element_type=jnp.float32)
        activated, gelu_slope = gelu_parts(pre_act)
        hidden = activated.astype(jnp.bfloat16)
        mixed_part = jnp.dot(hidden, w_down, preferred_element_type=jnp.float32)
        outputs = tok_rows.astype(jnp.float32) + mixed_part
        pooled_rows = lax.optimization_barrier(jnp.mean(outputs.reshape(K_DEV, P_SIZE, D), axis=1)).astype(jnp.bfloat16)
        learn_hat = unit_rows(jnp.dot(pooled_rows, ref_proj, preferred_element_type=jnp.float32))
        grad_act = jnp.dot(weighted, w_down.T, preferred_element_type=jnp.float32)
        grad_pre = (grad_act * gelu_slope).astype(jnp.bfloat16)
        grad_up = total_up + jnp.dot(tok_rows.T, grad_pre, preferred_element_type=jnp.float32)
        return (grad_up, learn_hat)
    zeros_grad = jnp.zeros((D, FF), jnp.float32)
    grad_up, learn_hat = lax.scan(learner_step, zeros_grad, (kept_tok, kept_cot, row_weight.reshape(n_sel, K_DEV)))
    learner_loss = lax.map(loss_block, (learn_hat, kept_global.reshape(n_sel, K_DEV))).reshape(KEPT)
    learnability = learner_loss - ref_loss[kept_global]
    return (ref_loss, learnability, grad_up)
```

```python
import jax
import jax.numpy as jnp
from jax import lax
from jax.sharding import PartitionSpec as P

logit_scale = 64.0
eps = 1e-06


def gelu_parts(pre_act):
    cumul = 0.5 * (1.0 + lax.erf(pre_act * 0.7071067811865476))
    density = jnp.exp(-0.5 * pre_act * pre_act) * 0.3989422804014327
    return (pre_act * cumul, cumul + pre_act * density)


def partial_scores(rows_hat, text_all):
    return lax.dot_general(
        rows_hat, text_all, (((1,), (1,)), ((), ())), preferred_element_type=jnp.float32
    )


def exp_total(rows_full, text_share):
    return jnp.sum(jnp.exp(logit_scale * partial_scores(rows_full, text_share)), axis=1)


def own_product(rows_part, texts_part):
    return jnp.sum(rows_part.astype(jnp.float32) * texts_part.astype(jnp.float32), axis=1)


def learn(kept_tok, kept_cot, row_weight, w_up, w_down, ref_proj):
    n_patch, n_items, d_part = kept_tok.shape
    n_rows = n_items * n_patch
    tok_full = lax.all_gather(kept_tok.reshape(n_rows, d_part), "mdl", axis=1, tiled=True)
    cot_full = lax.all_gather(kept_cot.reshape(n_rows, d_part), "mdl", axis=1, tiled=True)
    pre_act = jnp.dot(tok_full, w_up, preferred_element_type=jnp.float32)
    activated, gelu_slope = gelu_parts(pre_act)
    hidden = activated.astype(jnp.bfloat16).reshape(n_patch, n_items, -1)
    hidden_mean = jnp.mean(hidden, axis=0, dtype=jnp.float32).astype(jnp.bfloat16)
    mixed_part = jnp.dot(hidden_mean, w_down, preferred_element_type=jnp.float32)
    summed = lax.psum_scatter(mixed_part, "mdl", scatter_dimension=1, tiled=True)
    tok_mean = jnp.mean(kept_tok, axis=0, dtype=jnp.float32)
    pooled = (summed + tok_mean).astype(jnp.bfloat16)
    pooled_full = lax.all_gather(pooled, "mdl", axis=1, tiled=True)
    learn_emb = jnp.dot(pooled_full, ref_proj, preferred_element_type=jnp.float32)
    learn_sq = lax.psum(jnp.sum(learn_emb * learn_emb, axis=1), "mdl")
    learn_hat = (learn_emb * lax.rsqrt(learn_sq + eps)[:, None]).astype(jnp.bfloat16)
    grad_act = lax.dot_general(
        cot_full, w_down, (((1,), (1,)), ((), ())), preferred_element_type=jnp.float32
    )
    row_w = jnp.tile(row_weight, n_patch)[:, None]
    grad_pre = (grad_act * row_w * gelu_slope).astype(jnp.bfloat16)
    grad_part = lax.dot_general(
        tok_full, grad_pre, (((0,), (0,)), ((), ())), preferred_element_type=jnp.float32
    ).astype(jnp.bfloat16)
    grad_up = lax.psum_scatter(grad_part, "sel", scatter_dimension=0, tiled=True)
    return (learn_hat, grad_up.astype(jnp.float32))


def per_device(patches, text, ref_proj, w_up, w_down, kept_index, dest, cotan):
    n_sel = lax.axis_size("sel")
    ex_dev = text.shape[0]
    d_part = patches.shape[1]
    n_patch = patches.shape[0] // ex_dev
    k_dev = kept_index.shape[0]
    blocks = patches.reshape(ex_dev, n_patch, d_part)
    pooled = jnp.mean(blocks, axis=1, dtype=jnp.float32).astype(jnp.bfloat16)
    pooled_full = lax.all_gather(pooled, "mdl", axis=1, tiled=True)
    img_emb = jnp.dot(pooled_full, ref_proj, preferred_element_type=jnp.float32)
    text_vals = text.astype(jnp.float32)
    img_sq, text_sq = lax.psum(
        (jnp.sum(img_emb * img_emb, axis=1), jnp.sum(text_vals * text_vals, axis=1)), "mdl"
    )
    img_hat = (img_emb * lax.rsqrt(img_sq + eps)[:, None]).astype(jnp.bfloat16)
    text_hat = (text_vals * lax.rsqrt(text_sq + eps)[:, None]).astype(jnp.bfloat16)
    text_rows = lax.all_to_all(text_hat, "mdl", split_axis=0, concat_axis=1, tiled=True)
    text_split = lax.all_gather(text_rows, "sel", axis=0, tiled=True)
    img_full = lax.all_gather(img_hat, "mdl", axis=1, tiled=True)
    ref_total, ref_own = lax.psum(
        (exp_total(img_full, text_split), own_product(img_hat, text_hat)), "mdl"
    )
    ref_loss = jnp.log(ref_total) - logit_scale * ref_own
    kept_tok = blocks[kept_index].transpose(1, 0, 2)
    kept_cot = cotan.reshape(k_dev, n_patch, d_part).transpose(1, 0, 2)
    onehot = (dest[:, None] == jnp.arange(n_sel, dtype=jnp.int32)[None, :]).astype(jnp.float32)
    counts = lax.psum(jnp.sum(onehot, axis=0), "sel")
    row_weight = 1.0 / jnp.sum(onehot * counts[None, :], axis=1)
    kept_hat, grad_up = learn(kept_tok, kept_cot, row_weight, w_up, w_down, ref_proj)
    learn_full = lax.all_gather(kept_hat, "mdl", axis=1, tiled=True)
    learn_total, learn_own = lax.psum(
        (exp_total(learn_full, text_split), own_product(kept_hat, text_hat[kept_index])), "mdl"
    )
    learner_loss = jnp.log(learn_total) - logit_scale * learn_own
    learnability = learner_loss - ref_loss[kept_index]
    return (ref_loss, learnability, grad_up)


def solution(mesh):
    in_specs = (
        P("sel", "mdl"),
        P("sel", "mdl"),
        P(None, "mdl"),
        P(None, "mdl"),
        P("mdl", None),
        P("sel"),
        P("sel"),
        P("sel", "mdl"),
    )
    out_specs = (P("sel"), P("sel"), P("sel", "mdl"))
    return jax.shard_map(
        per_device, mesh=mesh, in_specs=in_specs, out_specs=out_specs, check_vma=False
    )
```

```python
import jax
import jax.numpy as jnp
from jax import lax
from jax.experimental import pallas as pl
from jax.experimental.pallas import tpu as pltpu
from jax.sharding import PartitionSpec as P

logit_scale = 64.0
eps = 1e-06
MESH = pl.DeviceIdType.MESH
f32 = jnp.float32
bf16 = jnp.bfloat16

NX, NY, NZ, NC = 4, 4, 8, 2
D, DP = 1408, 352
FH = 768
EMB, EP = 1024, 256
PATCH, E, K = 6, 128, 64
R = K * PATCH
G = 384
CH = 48
CA = 384
TB = E // NX

POS = {0: 0, 1: 1, 7: 2, 2: 3, 6: 4, 3: 5, 5: 6, 4: 7}
GROUPS = [(0, 1), (1, 2), (3, 2), (5, 2), (7, 1)]

N_COPIES = 112
N_LOCAL = 3


def dot(a, b):
    return lax.dot_general(a, b, (((1,), (0,)), ((), ())), preferred_element_type=f32)


def dot_nt(a, b):
    return lax.dot_general(a, b, (((1,), (1,)), ((), ())), preferred_element_type=f32)


def iota(shape, axis):
    return lax.broadcasted_iota(jnp.int32, shape, axis)


def one_hot(mask):
    return jnp.where(mask, 1.0, 0.0).astype(bf16)


def pool_mask(n_out, n_in):
    first = PATCH * iota((n_out, n_in), 0)
    col = iota((n_out, n_in), 1)
    return (col >= first) & (col < first + PATCH)


def spread(row):
    first = PATCH * iota((R, K), 1)
    line = iota((R, K), 0)
    return jnp.sum(jnp.where((line >= first) & (line < first + PATCH), row, 0.0), axis=1, keepdims=True)


def to_row(col, lanes):
    n = col.shape[0]
    return jnp.sum(jnp.where(iota((n, lanes), 0) == iota((n, lanes), 1), col, 0.0), axis=0, keepdims=True)


def to_col(row, n):
    lanes = row.shape[1]
    return jnp.sum(jnp.where(iota((n, lanes), 0) == iota((n, lanes), 1), row, 0.0), axis=1, keepdims=True)


SCRATCH = dict(
    proj=((D, EP), bf16),
    wup=((D, FH), bf16),
    wdn=((FH, D), bf16),
    wdt=((D, FH), bf16),
    tok=((2, NX, R, DP), bf16),
    cot=((2, NX, R, DP), bf16),
    pre=((2, R, FH), f32),
    act=((2, R, FH), f32),
    hid=((2 * R, FH), bf16),
    tokt=((NX, G, 2 * R), bf16),
    gpre=((2 * R, FH), bf16),
    tx=((NX, TB, EP), bf16),
    txt=((2 * NY, NZ * TB, EMB), bf16),
    dst=((2, 8, 128), f32),
    hz=((NZ, 8, 128), f32),
    hy=((NY, 8, 128), f32),
    mb=((2, NX, K, DP), f32),
    mr=((NX, K, DP), f32),
    mx=((NX, K, DP), f32),
    mxr=((NX, K, DP), f32),
    lpb=((NX, K, DP), bf16),
    leb=((NX, K, EP), bf16),
    lhat=((K, EMB), bf16),
    pb=((NX, E, DP), bf16),
    eb=((NX, E, EP), bf16),
    ihat=((E, EMB), bf16),
    rs=((NX, 8, 128), f32),
    ls=((NX, 8, 128), f32),
    ga=((NY, G, CA), f32),
    gb=((NY, G, FH - CA), f32),
    a1=((G, CA), f32),
    b1=((NY, CH, FH - CA), f32),
    sbp=((4, NY, CH, FH - CA), bf16),
    sbm=((4, NY, CH, FH - CA), bf16),
    rbp=((4, NY, CH, FH - CA), bf16),
    rbm=((4, NY, CH, FH - CA), bf16),
    sap=((2, G, CA), bf16),
    sam=((2, G, CA), bf16),
    rap=((2, G, CA), bf16),
    ram=((2, G, CA), bf16),
    szp=((4, CH, CA), bf16),
    szm=((3, CH, CA), bf16),
    rzp=((4, CH, CA), bf16),
    rzm=((3, CH, CA), bf16),
    syp=((2, CH, FH - CA), bf16),
    sym=((1, CH, FH - CA), bf16),
    ryp=((2, CH, FH - CA), bf16),
    rym=((1, CH, FH - CA), bf16),
    res=((CH, FH), f32),
    fin=((CH // 2, FH), f32),
)


def kernel(patches, text, cotan, kidx, dest, proj_hbm, wup_hbm, wdn_hbm, ref_out, learn_out, grad_out, *scratch):
    names = list(SCRATCH)
    s = dict(zip(names, scratch[: len(names)]))
    send_sem, recv_sem, local_sem = scratch[len(names) :]

    x = lax.axis_index("mdl")
    sel = lax.axis_index("sel")
    c = lax.rem(sel, NC)
    z = lax.rem(lax.div(sel, NC), NZ)
    y = lax.div(sel, NC * NZ)

    def dev(dx=0, dy=0, dz=0, dc=0):
        yy = lax.rem(y + dy, NY)
        zz = lax.rem(z + dz, NZ)
        cc = lax.rem(c + dc, NC)
        return {"sel": (yy * NZ + zz) * NC + cc, "mdl": lax.rem(x + dx, NX)}

    sib = dev(dc=1)
    xr = [None] + [dev(dx=r) for r in range(1, NX)]
    yp, ym, zp, zm = dev(dy=1), dev(dy=NY - 1), dev(dz=1), dev(dz=NZ - 1)
    partners = [sib, xr[1], xr[2], xr[3], yp, ym, zp, zm]

    copies = []

    def send(src, dst, device):
        i = len(copies)
        copy = pltpu.make_async_remote_copy(
            src_ref=src,
            dst_ref=dst,
            send_sem=send_sem.at[i],
            recv_sem=recv_sem.at[i],
            device_id=device,
            device_id_type=MESH,
        )
        copy.start()
        copies.append(copy)
        return copy

    def xblock(slot):
        return pl.ds(pl.multiple_of(lax.rem(x + NX - slot, NX) * DP, 32), DP)

    barrier = pltpu.get_barrier_semaphore()
    for p in partners:
        pl.semaphore_signal(barrier, inc=1, device_id=p, device_id_type=MESH)
    half = pl.multiple_of(c * FH, FH)
    loads = [
        pltpu.make_async_copy(wdn_hbm.at[pl.ds(half, FH), :], s["wdn"], local_sem.at[0]),
        pltpu.make_async_copy(wup_hbm.at[:, pl.ds(half, FH)], s["wup"], local_sem.at[1]),
        pltpu.make_async_copy(proj_hbm, s["proj"], local_sem.at[2]),
    ]
    for load in loads:
        load.start()

    kf = kidx[...].astype(f32)
    krow = spread(kf)
    line = iota((R, 1), 0).astype(f32)
    entry = spread(iota((1, K), 1).astype(f32))
    want = (PATCH * krow + (line - PATCH * entry)).astype(jnp.int32)
    s["tok"][0, 0] = dot(one_hot(iota((R, E * PATCH), 1) == want), patches[...]).astype(bf16)
    s["cot"][0, 0] = cotan[...]
    s["dst"][0] = jnp.zeros((8, 128), f32)
    s["dst"][0, 0:1, 0:K] = dest[...].astype(f32)

    pl.semaphore_wait(barrier, len(partners))

    text_cp = [
        send(text.at[pl.ds(pl.multiple_of(lax.rem(x + r, NX) * TB, TB), TB), :], s["tx"].at[r], xr[r])
        for r in range(1, NX)
    ]
    dst_cp = send(s["dst"].at[0], s["dst"].at[1], sib)

    def ring_start(buf):
        return (
            send(buf.at[0, 0], buf.at[0, 1], xr[1]),
            send(buf.at[0, 0], buf.at[0, 3], xr[3]),
            send(buf.at[0, 0], buf.at[1, 0], sib),
        )

    def ring_forward(buf, first):
        first[0].wait_recv()
        first[1].wait_recv()
        return (
            send(buf.at[0, 1, pl.ds(0, R // 2), :], buf.at[0, 2, pl.ds(0, R // 2), :], xr[1]),
            send(buf.at[0, 3, pl.ds(R // 2, R // 2), :], buf.at[0, 2, pl.ds(R // 2, R // 2), :], xr[3]),
        )

    tok1 = ring_start(s["tok"])

    loads[0].wait()
    eye = one_hot(iota((128, 128), 0) == iota((128, 128), 1))
    for j in range(D // 128):
        s["wdt"][j * 128 : (j + 1) * 128, :] = dot_nt(eye, s["wdn"][:, j * 128 : (j + 1) * 128]).astype(bf16)
    loads[1].wait()

    s["tx"][0] = text[pl.ds(pl.multiple_of(x * TB, TB), TB), :]
    for cp in text_cp:
        cp.wait_recv()
    tv = [s["tx"][r].astype(f32) for r in range(NX)]
    tsq = sum(jnp.sum(v * v, axis=1, keepdims=True) for v in tv)
    tinv = lax.rsqrt(tsq + eps)
    for r in range(NX):
        s["txt"][0, 0:TB, r * EP : (r + 1) * EP] = (tv[r] * tinv).astype(bf16)

    dst_cp.wait_recv()
    lane = iota((K, 128), 1).astype(f32)
    chip_hist = jnp.zeros((1, 128), f32)
    for sh in range(2):
        dcol = to_col(s["dst"][sh, 0:1, :], K)
        chip_hist += jnp.sum(jnp.where(lane == dcol, 1.0, 0.0), axis=0, keepdims=True)
    s["hz"][0] = jnp.broadcast_to(chip_hist, (8, 128))

    def tz(slot):
        return s["txt"].at[0, pl.ds(POS[slot] * TB, TB), :]

    def z_step(t):
        out = [
            (send(tz(t - 1), tz(t), zp), send(s["hz"].at[t - 1], s["hz"].at[t], zp)),
        ]
        if t < NZ // 2:
            a, b = (NZ - t + 1) % NZ, NZ - t
            out.append((send(tz(a), tz(b), zm), send(s["hz"].at[a], s["hz"].at[b], zm)))
        return out

    def z_wait(step):
        for cp, hcp in step:
            cp.wait_recv()
            hcp.wait_recv()

    def yg(slot, g):
        first, n = GROUPS[g]
        return s["txt"].at[slot, pl.ds(first * TB, n * TB), :]

    def y_first(g):
        return (send(yg(0, g), yg(1, g), yp), send(yg(0, g), yg(3, g), ym))

    zs1 = z_step(1)
    ys = [y_first(0)]

    def up(sh, slot):
        part = dot(s["tok"][sh, slot], s["wup"][xblock(slot), :])
        s["pre"][sh] = part if slot == 0 else s["pre"][sh] + part

    up(0, 0)
    z_wait(zs1)
    zs2 = z_step(2)
    ys.append(y_first(1))
    tok1[2].wait_recv()
    up(1, 0)
    s["pb"][0] = (dot(one_hot(pool_mask(E, E * PATCH)), patches[...]) * (1.0 / PATCH)).astype(bf16)
    z_wait(zs2)
    zs3 = z_step(3)
    ys.append(y_first(2))

    tok2 = ring_forward(s["tok"], tok1)
    cot1 = ring_start(s["cot"])
    tokc = [send(s["tok"].at[0, i], s["tok"].at[1, i], sib) for i in (1, 3)]
    up(0, 1)
    z_wait(zs3)
    zs4 = z_step(4)
    ys.append(y_first(3))
    up(0, 3)
    tokc[0].wait_recv()
    up(1, 1)
    tokc[1].wait_recv()
    up(1, 3)
    z_wait(zs4)
    ys.append(y_first(4))
    txt_c = [send(s["txt"].at[0], s["txt"].at[NY], sib)]
    s["hy"][0] = sum(s["hz"][i] for i in range(NZ))
    hy1 = (send(s["hy"].at[0], s["hy"].at[1], yp), send(s["hy"].at[0], s["hy"].at[3], ym))

    tok2[0].wait_recv()
    tok2[1].wait_recv()
    tokc2 = send(s["tok"].at[0, 2], s["tok"].at[1, 2], sib)
    up(0, 2)
    tokc2.wait_recv()
    up(1, 2)

    for sh in range(2):

        def act_step(i, carry):
            rows = pl.ds(pl.multiple_of(i * 32, 32), 32)
            v = s["pre"][sh, rows, :]
            cumul = 0.5 * (1.0 + lax.erf(v * 0.7071067811865476))
            density = jnp.exp(-0.5 * v * v) * 0.3989422804014327
            s["hid"][pl.ds(pl.multiple_of(sh * R + i * 32, 32), 32), :] = (v * cumul).astype(bf16)
            s["pre"][sh, rows, :] = cumul + v * density
            return carry

        lax.fori_loop(0, R // 32, act_step, 0)

    gi, gj = iota((G, DP), 0), iota((G, DP), 1)
    base = 22 * lax.div(gi, 24)
    inner = lax.rem(gi, 24)
    place = one_hot((inner < 22) & (gj == base + inner))
    for slot in range(NX):
        for sh in range(2):
            s["tokt"][slot, :, sh * R : (sh + 1) * R] = dot_nt(place, s["tok"][sh, slot]).astype(bf16)

    hy1[0].wait_recv()
    hy1[1].wait_recv()
    hy2 = send(s["hy"].at[1], s["hy"].at[2], yp)
    for g in range(5):
        ys[g][0].wait_recv()
        ys[g][1].wait_recv()
    ys2 = [send(yg(1, g), yg(2, g), yp) for g in (0, 1, 4)]
    ys2 += [send(yg(3, g), yg(2, g), ym) for g in (2, 3)]
    txt_c += [send(s["txt"].at[i], s["txt"].at[NY + i], sib) for i in (1, 3)]

    pooled_h = dot(one_hot(pool_mask(2 * K, 2 * R)), s["hid"][...]) * (1.0 / PATCH)
    pooled_h = pooled_h.astype(bf16)
    for slot in range(NX):
        m = dot_nt(pooled_h, s["wdt"][xblock(slot), :])
        s["mb"][0, slot] = m[0:K]
        s["mb"][1, slot] = m[K : 2 * K]
    m_c = send(s["mb"].at[1], s["mr"], sib)

    def back(sh, slot):
        part = dot(s["cot"][sh, slot], s["wdt"][xblock(slot), :])
        s["act"][sh] = part if slot == 0 else s["act"][sh] + part

    back(0, 0)
    cot1[2].wait_recv()
    back(1, 0)
    cot2 = ring_forward(s["cot"], cot1)
    cotc = [send(s["cot"].at[0, i], s["cot"].at[1, i], sib) for i in (1, 3)]
    pb_cp = [send(s["pb"].at[0], s["pb"].at[r], xr[r]) for r in range(1, NX)]
    back(0, 1)
    back(0, 3)
    cotc[0].wait_recv()
    back(1, 1)
    cotc[1].wait_recv()
    back(1, 3)

    hy2.wait_recv()
    counts = sum(s["hy"][i][0:1, :] for i in range(NY))
    lane_r = iota((R, 128), 1).astype(f32)
    weight = []
    for sh in range(2):
        drow = spread(s["dst"][sh, 0:1, 0:K])
        weight.append(1.0 / jnp.sum(jnp.where(lane_r == drow, counts, 0.0), axis=1, keepdims=True))

    m_c.wait_recv()
    for slot in range(NX):
        s["mx"][slot] = s["mb"][0, slot] + s["mr"][slot]
    mx_cp = [send(s["mx"].at[NX - r], s["mxr"].at[r], xr[r]) for r in range(1, NX)]

    cot2[0].wait_recv()
    cot2[1].wait_recv()
    cotc2 = send(s["cot"].at[0, 2], s["cot"].at[1, 2], sib)
    back(0, 2)
    cotc2.wait_recv()
    back(1, 2)
    for sh in range(2):
        s["gpre"][sh * R : (sh + 1) * R, :] = (s["act"][sh] * weight[sh] * s["pre"][sh]).astype(bf16)

    def slot_of(delta):
        return lax.rem(x + 2 * NY - y - delta, NX)

    def zrows(zeta):
        return pl.ds(pl.multiple_of(lax.rem(z + zeta, NZ) * CH, 16), CH)

    for delta in range(NY):
        s["gb"][delta] = dot(s["tokt"][slot_of(delta)], s["gpre"][:, CA:FH])

    def b_step(t, before):
        sp, sm, rp, rm = s["sbp"], s["sbm"], s["rbp"], s["rbm"]
        if t == 1:
            for delta in (0, 1):
                sp[0, delta] = s["gb"][delta, zrows(4), :].astype(bf16)
            for delta in (2, 3):
                sm[0, delta] = s["gb"][delta, zrows(4), :].astype(bf16)
            return (
                send(sp.at[0, pl.ds(0, 2)], rp.at[0, pl.ds(0, 2)], zp),
                send(sm.at[0, pl.ds(2, 2)], rm.at[0, pl.ds(2, 2)], zm),
            )
        before[0].wait_recv()
        before[1].wait_recv()
        for delta in range(NY):
            vp = s["gb"][delta, zrows(5 - t), :]
            vm = s["gb"][delta, zrows(3 + t), :]
            if t > 2 or delta < 2:
                vp = vp + rp[t - 2, delta].astype(f32)
            if t > 2 or delta >= 2:
                vm = vm + rm[t - 2, delta].astype(f32)
            sp[t - 1, delta] = vp.astype(bf16)
            sm[t - 1, delta] = vm.astype(bf16)
        return send(sp.at[t - 1], rp.at[t - 1], zp), send(sm.at[t - 1], rm.at[t - 1], zm)

    bs = b_step(1, None)

    def ga(delta):
        s["ga"][delta] = dot(s["tokt"][slot_of(delta)], s["gpre"][:, 0:CA])

    ga(2)
    hg = G // 2
    s["sap"][0, 0:hg, :] = s["ga"][2, 0:hg, :].astype(bf16)
    s["sam"][0, hg:G, :] = s["ga"][2, hg:G, :].astype(bf16)
    as1 = (
        send(s["sap"].at[0, pl.ds(0, hg)], s["rap"].at[0, pl.ds(0, hg)], yp),
        send(s["sam"].at[0, pl.ds(hg, hg)], s["ram"].at[0, pl.ds(hg, hg)], ym),
    )
    ga(1)
    ga(3)
    ga(0)

    for cp in ys2:
        cp.wait_recv()
    txt_c.append(send(s["txt"].at[2], s["txt"].at[NY + 2], sib))

    bs = b_step(2, bs)

    for cp in mx_cp:
        cp.wait_recv()
    tok_mean = dot(one_hot(pool_mask(K, R)), s["tok"][0, 0]) * (1.0 / PATCH)
    mixed = s["mx"][0] + s["mxr"][1] + s["mxr"][2] + s["mxr"][3]
    s["lpb"][0] = (tok_mean + mixed).astype(bf16)
    lp_cp = [send(s["lpb"].at[0], s["lpb"].at[r], xr[r]) for r in range(1, NX)]

    as1[0].wait_recv()
    as1[1].wait_recv()
    s["sap"][1, 0:hg, :] = (s["ga"][1, 0:hg, :] + s["rap"][0, 0:hg, :].astype(f32)).astype(bf16)
    s["sap"][1, hg:G, :] = s["ga"][1, hg:G, :].astype(bf16)
    s["sam"][1, 0:hg, :] = s["ga"][3, 0:hg, :].astype(bf16)
    s["sam"][1, hg:G, :] = (s["ga"][3, hg:G, :] + s["ram"][0, hg:G, :].astype(f32)).astype(bf16)
    as2 = (send(s["sap"].at[1], s["rap"].at[1], yp), send(s["sam"].at[1], s["ram"].at[1], ym))

    loads[2].wait()
    for cp in pb_cp:
        cp.wait_recv()
    emb = sum(dot(s["pb"][slot], s["proj"][xblock(slot), :]) for slot in range(NX))
    s["eb"][0] = emb.astype(bf16)
    eb_cp = [send(s["eb"].at[0], s["eb"].at[r], xr[r]) for r in range(1, NX)]

    bs = b_step(3, bs)

    for cp in lp_cp:
        cp.wait_recv()
    emb = sum(dot(s["lpb"][slot], s["proj"][xblock(slot), :]) for slot in range(NX))
    s["leb"][0] = emb.astype(bf16)
    le_cp = [send(s["leb"].at[0], s["leb"].at[r], xr[r]) for r in range(1, NX)]

    def normalise(blocks, out):
        v = [blocks[slot].astype(f32) for slot in range(NX)]
        inv = lax.rsqrt(sum(jnp.sum(e * e, axis=1, keepdims=True) for e in v) + eps)
        for slot in range(NX):
            out[:, slot * EP : (slot + 1) * EP] = (v[slot] * inv).astype(bf16)

    def exp_total(hat):
        n = hat.shape[0]

        def step(i, acc):
            return acc + jnp.exp(logit_scale * dot_nt(hat[...], s["txt"][i]))

        acc = lax.fori_loop(0, 2 * NY, step, jnp.zeros((n, NZ * TB), f32))
        return jnp.sum(acc, axis=1, keepdims=True)

    def own_product(hat, own_col):
        scores = dot_nt(hat[...], s["txt"][0, 0:TB, :])
        mine = own_col == (iota(scores.shape, 1) + x * TB)
        return jnp.sum(jnp.where(mine, scores, 0.0), axis=1, keepdims=True)

    def share(buf, total, own):
        buf[0] = jnp.zeros((8, 128), f32)
        buf[0, 0:1, :] = to_row(total, 128)
        buf[0, 1:2, :] = to_row(own, 128)
        return [send(buf.at[0], buf.at[r], xr[r]) for r in range(1, NX)]

    def loss_row(buf, cps):
        for cp in cps:
            cp.wait_recv()
        tile = buf[0] + buf[1] + buf[2] + buf[3]
        return jnp.log(tile[0:1, :]) - logit_scale * tile[1:2, :]

    for cp in eb_cp:
        cp.wait_recv()
    normalise(s["eb"], s["ihat"])
    for cp in txt_c:
        cp.wait_recv()
    r_cp = share(s["rs"], exp_total(s["ihat"]), own_product(s["ihat"], iota((E, 1), 0)))

    bs = b_step(4, bs)

    as2[0].wait_recv()
    as2[1].wait_recv()
    s["a1"][...] = s["ga"][0] + s["rap"][1].astype(f32) + s["ram"][1].astype(f32)

    def a_step(t, before):
        vp = s["a1"][zrows(5 - t), :]
        if t > 1:
            before[0].wait_recv()
            vp = vp + s["rzp"][t - 2].astype(f32)
        s["szp"][t - 1] = vp.astype(bf16)
        out = [send(s["szp"].at[t - 1], s["rzp"].at[t - 1], zp)]
        if t < 4:
            vm = s["a1"][zrows(4 + t), :]
            if t > 1:
                before[1].wait_recv()
                vm = vm + s["rzm"][t - 2].astype(f32)
            s["szm"][t - 1] = vm.astype(bf16)
            out.append(send(s["szm"].at[t - 1], s["rzm"].at[t - 1], zm))
        return out

    az1 = a_step(1, None)

    for cp in le_cp:
        cp.wait_recv()
    normalise(s["leb"], s["lhat"])
    kcol = to_col(kf, K)
    l_cp = share(s["ls"], exp_total(s["lhat"]), own_product(s["lhat"], kcol.astype(jnp.int32)))

    az2 = a_step(2, az1)

    bs[0].wait_recv()
    bs[1].wait_recv()
    for delta in range(NY):
        s["b1"][delta] = s["gb"][delta, zrows(0), :] + s["rbp"][3, delta].astype(f32) + s["rbm"][3, delta].astype(f32)
    s["syp"][0] = s["b1"][2].astype(bf16)
    s["sym"][0] = s["b1"][3].astype(bf16)
    by1 = (send(s["syp"].at[0], s["ryp"].at[0], yp), send(s["sym"].at[0], s["rym"].at[0], ym))

    az3 = a_step(3, az2)

    by1[0].wait_recv()
    s["syp"][1] = (s["b1"][1] + s["ryp"][0].astype(f32)).astype(bf16)
    by2 = send(s["syp"].at[1], s["ryp"].at[1], yp)

    az4 = a_step(4, az3)

    ref_row = loss_row(s["rs"], r_cp)
    ref_out[...] = ref_row
    learn_row = loss_row(s["ls"], l_cp)
    picked = jnp.sum(jnp.where(iota((K, E), 1).astype(f32) == kcol, ref_row, 0.0), axis=1, keepdims=True)
    learn_out[...] = learn_row[:, 0:K] - to_row(picked, K)

    by1[1].wait_recv()
    by2.wait_recv()
    s["res"][:, CA:FH] = s["b1"][0] + s["ryp"][1].astype(f32) + s["rym"][0].astype(f32)
    az3[1].wait_recv()
    az4[0].wait_recv()
    s["res"][:, 0:CA] = s["a1"][zrows(0), :] + s["rzp"][3].astype(f32) + s["rzm"][2].astype(f32)

    other = pl.ds(pl.multiple_of((1 - c) * (CH // 2), 8), CH // 2)
    fin = send(s["res"].at[other, :], s["fin"], sib)
    mine = s["res"][pl.ds(pl.multiple_of(c * (CH // 2), 8), CH // 2), :][0:22, :]
    fin.wait_recv()
    theirs = s["fin"][0:22, :]
    grad_out[:, 0:FH] = jnp.where(c == 0, mine, theirs)
    grad_out[:, FH : 2 * FH] = jnp.where(c == 0, theirs, mine)

    for cp in copies:
        cp.wait_send()


def per_device(patches, text, ref_proj, w_up, w_down, kept_index, dest, cotan):
    vmem = pl.BlockSpec(memory_space=pltpu.VMEM)
    hbm = pl.BlockSpec(memory_space=pl.ANY)
    scratch = [pltpu.VMEM(shape, dtype) for shape, dtype in SCRATCH.values()]
    scratch += [
        pltpu.SemaphoreType.DMA((N_COPIES,)),
        pltpu.SemaphoreType.DMA((N_COPIES,)),
        pltpu.SemaphoreType.DMA((N_LOCAL,)),
    ]
    ref_loss, learnability, grad_up = pl.pallas_call(
        kernel,
        out_shape=(
            jax.ShapeDtypeStruct((1, E), f32),
            jax.ShapeDtypeStruct((1, K), f32),
            jax.ShapeDtypeStruct((22, 2 * FH), f32),
        ),
        in_specs=[vmem] * 5 + [hbm] * 3,
        out_specs=(vmem, vmem, vmem),
        scratch_shapes=scratch,
        compiler_params=pltpu.CompilerParams(
            collective_id=0, has_side_effects=True, vmem_limit_bytes=56 * 1024 * 1024
        ),
        name="contrastive_step",
    )(patches, text, cotan, kept_index.reshape(1, K), dest.reshape(1, K), ref_proj, w_up, w_down)
    return (ref_loss.reshape(E), learnability.reshape(K), grad_up)


def solution(mesh):
    in_specs = (
        P("sel", "mdl"),
        P("sel", "mdl"),
        P(None, "mdl"),
        P(None, "mdl"),
        P("mdl", None),
        P("sel"),
        P("sel"),
        P("sel", "mdl"),
    )
    out_specs = (P("sel"), P("sel"), P("sel", "mdl"))
    return jax.shard_map(
        per_device, mesh=mesh, in_specs=in_specs, out_specs=out_specs, check_vma=False
    )
```

```python
import jax
import jax.numpy as jnp
from jax import lax
from jax.experimental import pallas as pl
from jax.experimental.pallas import tpu as pltpu
from jax.sharding import PartitionSpec as P

logit_scale = 64.0
eps = 1e-06
MESH = pl.DeviceIdType.MESH
f32 = jnp.float32
bf16 = jnp.bfloat16

NX, NY, NZ, NC = 4, 4, 8, 2
D, DP = 1408, 352
FH = 768
EMB, EP = 1024, 256
PATCH, E, K = 6, 128, 64
R = K * PATCH
G = 384
CH = 48
CA = 384
TB = E // NX

POS = {0: 0, 1: 1, 7: 2, 2: 3, 6: 4, 3: 5, 5: 6, 4: 7}
GROUPS = [(0, 1), (1, 2), (3, 2), (5, 2), (7, 1)]

N_COPIES = 150
N_LOCAL = 3


def dot(a, b):
    return lax.dot_general(a, b, (((1,), (0,)), ((), ())), preferred_element_type=f32)


def dot_tn(a, b):
    return lax.dot_general(a, b, (((0,), (0,)), ((), ())), preferred_element_type=f32)


def dot_nt(a, b):
    return lax.dot_general(a, b, (((1,), (1,)), ((), ())), preferred_element_type=f32)


def iota(shape, axis):
    return lax.broadcasted_iota(jnp.int32, shape, axis)


def one_hot(mask):
    return jnp.where(mask, 1.0, 0.0).astype(bf16)


def pool_mask(n_out, n_in):
    first = PATCH * iota((n_out, n_in), 0)
    col = iota((n_out, n_in), 1)
    return (col >= first) & (col < first + PATCH)


def spread(row):
    first = PATCH * iota((R, K), 1)
    line = iota((R, K), 0)
    return jnp.sum(jnp.where((line >= first) & (line < first + PATCH), row, 0.0), axis=1, keepdims=True)


def to_row(col, lanes):
    n = col.shape[0]
    return jnp.sum(jnp.where(iota((n, lanes), 0) == iota((n, lanes), 1), col, 0.0), axis=0, keepdims=True)


def to_col(row, n):
    lanes = row.shape[1]
    return jnp.sum(jnp.where(iota((n, lanes), 0) == iota((n, lanes), 1), row, 0.0), axis=1, keepdims=True)


SCRATCH = dict(
    proj=((D, EP), bf16),
    wup=((D, FH), bf16),
    wdn=((FH, D), bf16),
    wdt=((D, FH), bf16),
    tok=((2, NX, DP, R), bf16),
    cot=((2, NX, DP, R), bf16),
    pre=((2, R, FH), f32),
    act=((2, R, FH), f32),
    hid=((2 * R, FH), bf16),
    tokt=((NX, G, 2 * R), bf16),
    gpre=((2 * R, FH), bf16),
    tx=((NX, TB, EP), bf16),
    txt=((2 * NY, NZ * TB, EMB), bf16),
    dst=((2, 8, 128), f32),
    hz=((NZ, 8, 128), f32),
    hy=((NY, 8, 128), f32),
    mb=((2, NX, K, DP), f32),
    mr=((NX, K, DP), f32),
    mx=((NX, K, DP), f32),
    mxr=((NX, K, DP), f32),
    lpb=((NX, K, DP), bf16),
    leb=((NX, K, EP), bf16),
    lhat=((K, EMB), bf16),
    pb=((NX, E, DP), bf16),
    eb=((NX, E, EP), bf16),
    ihat=((E, EMB), bf16),
    rs=((NX, 8, 128), f32),
    ls=((NX, 8, 128), f32),
    ga=((NY, G, CA), f32),
    gb=((NY, G, FH - CA), f32),
    a1=((G, CA), f32),
    b1=((NY, CH, FH - CA), f32),
    sbp=((4, NY, CH, FH - CA), bf16),
    sbm=((4, NY, CH, FH - CA), bf16),
    rbp=((4, NY, CH, FH - CA), bf16),
    rbm=((4, NY, CH, FH - CA), bf16),
    sap=((2, G, CA), bf16),
    sam=((2, G, CA), bf16),
    rap=((2, G, CA), bf16),
    ram=((2, G, CA), bf16),
    sz=((NZ, CH, CA), bf16),
    rz=((NZ, CH, CA), bf16),
    sy=((NY, CH, FH - CA), bf16),
    ry=((NY, CH, FH - CA), bf16),
    res=((CH, FH), f32),
    fin=((CH // 2, FH), f32),
)


def kernel(patches, text, cotan, kidx, dest, proj_hbm, wup_hbm, wdn_hbm, loss_out, grad_out, *scratch):
    names = list(SCRATCH)
    s = dict(zip(names, scratch[: len(names)]))
    send_sem, recv_sem, local_sem = scratch[len(names) :]

    x = lax.axis_index("mdl")
    sel = lax.axis_index("sel")
    c = lax.rem(sel, NC)
    z = lax.rem(lax.div(sel, NC), NZ)
    y = lax.div(sel, NC * NZ)

    def dev(dx=0, dy=0, dz=0, dc=0):
        yy = lax.rem(y + dy, NY)
        zz = lax.rem(z + dz, NZ)
        cc = lax.rem(c + dc, NC)
        return {"sel": (yy * NZ + zz) * NC + cc, "mdl": lax.rem(x + dx, NX)}

    sib = dev(dc=1)
    xr = [None] + [dev(dx=r) for r in range(1, NX)]
    yr = [None] + [dev(dy=r) for r in range(1, NY)]
    zr = [None] + [dev(dz=r) for r in range(1, NZ)]
    yp, ym, zp, zm = yr[1], yr[NY - 1], zr[1], zr[NZ - 1]
    partners = [sib] + xr[1:] + yr[1:] + zr[1:]

    copies = []

    def send(src, dst, device):
        i = len(copies)
        copy = pltpu.make_async_remote_copy(
            src_ref=src,
            dst_ref=dst,
            send_sem=send_sem.at[i],
            recv_sem=recv_sem.at[i],
            device_id=device,
            device_id_type=MESH,
        )
        copy.start()
        copies.append(copy)
        return copy

    def xblock(slot):
        return pl.ds(pl.multiple_of(lax.rem(x + NX - slot, NX) * DP, 32), DP)

    barrier = pltpu.get_barrier_semaphore()
    for p in partners:
        pl.semaphore_signal(barrier, inc=1, device_id=p, device_id_type=MESH)
    half = pl.multiple_of(c * FH, FH)
    loads = [
        pltpu.make_async_copy(wdn_hbm.at[pl.ds(half, FH), :], s["wdn"], local_sem.at[0]),
        pltpu.make_async_copy(wup_hbm.at[:, pl.ds(half, FH)], s["wup"], local_sem.at[1]),
        pltpu.make_async_copy(proj_hbm, s["proj"], local_sem.at[2]),
    ]
    for load in loads:
        load.start()

    kf = kidx[...].astype(f32)
    krow = spread(kf)
    line = iota((R, 1), 0).astype(f32)
    entry = spread(iota((1, K), 1).astype(f32))
    want = (PATCH * krow + (line - PATCH * entry)).astype(jnp.int32)
    s["tok"][0, 0] = dot_nt(patches[...], one_hot(iota((R, E * PATCH), 1) == want)).astype(bf16)
    s["cot"][0, 0] = cotan[...]
    s["dst"][0] = jnp.zeros((8, 128), f32)
    s["dst"][0, 0:1, 0:K] = dest[...].astype(f32)

    pl.semaphore_wait(barrier, len(partners))

    text_cp = [
        send(text.at[pl.ds(pl.multiple_of(lax.rem(x + r, NX) * TB, TB), TB), :], s["tx"].at[r], xr[r])
        for r in range(1, NX)
    ]
    dst_cp = send(s["dst"].at[0], s["dst"].at[1], sib)

    h = DP // 2

    def half_to(buf, src, dst, part, device):
        rows = pl.ds(part * h, h)
        return send(buf.at[0, src, rows, :], buf.at[0, dst, rows, :], device)

    def ring_start(buf):
        first = (half_to(buf, 0, 1, 0, xr[1]), half_to(buf, 0, 3, 1, xr[3]))
        second = (half_to(buf, 0, 1, 1, xr[1]), half_to(buf, 0, 3, 0, xr[3]))
        return first, second

    def ring_forward(buf, first):
        out = []
        first[0].wait_recv()
        out.append(half_to(buf, 1, 2, 0, xr[1]))
        first[1].wait_recv()
        out.append(half_to(buf, 3, 2, 1, xr[3]))
        return out

    def wait_both(pair):
        pair[0].wait_recv()
        pair[1].wait_recv()

    def to_core(buf, slot):
        return send(buf.at[0, slot], buf.at[1, slot], sib)

    tok1 = ring_start(s["tok"])
    tokc0 = to_core(s["tok"], 0)
    cotc0 = to_core(s["cot"], 0)

    dst_cp.wait_recv()
    lane = iota((K, 128), 1).astype(f32)
    chip_hist = jnp.zeros((1, 128), f32)
    for sh in range(2):
        dcol = to_col(s["dst"][sh, 0:1, :], K)
        chip_hist += jnp.sum(jnp.where(lane == dcol, 1.0, 0.0), axis=0, keepdims=True)
    s["hz"][0] = jnp.broadcast_to(chip_hist, (8, 128))
    hz_cp = [send(s["hz"].at[0], s["hz"].at[r], zr[r]) for r in range(1, NZ)]

    loads[0].wait()
    eye = one_hot(iota((128, 128), 0) == iota((128, 128), 1))
    for j in range(D // 128):
        s["wdt"][j * 128 : (j + 1) * 128, :] = dot_nt(eye, s["wdn"][:, j * 128 : (j + 1) * 128]).astype(bf16)
    loads[1].wait()

    s["tx"][0] = text[pl.ds(pl.multiple_of(x * TB, TB), TB), :]
    for cp in text_cp:
        cp.wait_recv()
    tv = [s["tx"][r].astype(f32) for r in range(NX)]
    tsq = sum(jnp.sum(v * v, axis=1, keepdims=True) for v in tv)
    tinv = lax.rsqrt(tsq + eps)
    for r in range(NX):
        s["txt"][0, 0:TB, r * EP : (r + 1) * EP] = (tv[r] * tinv).astype(bf16)

    def tz(slot):
        return s["txt"].at[0, pl.ds(POS[slot] * TB, TB), :]

    def z_step(t):
        out = [send(tz(t - 1), tz(t), zp)]
        if t < NZ // 2:
            out.append(send(tz((NZ - t + 1) % NZ), tz(NZ - t), zm))
        return out

    def z_wait(step):
        for cp in step:
            cp.wait_recv()

    def yg(slot, g):
        first, n = GROUPS[g]
        return s["txt"].at[slot, pl.ds(first * TB, n * TB), :]

    def y_first(g):
        return (send(yg(0, g), yg(1, g), yp), send(yg(0, g), yg(3, g), ym))

    def up(sh, slot):
        part = dot_tn(s["tok"][sh, slot], s["wup"][xblock(slot), :])
        s["pre"][sh] = part if slot == 0 else s["pre"][sh] + part

    def back(sh, slot):
        part = dot_tn(s["cot"][sh, slot], s["wdt"][xblock(slot), :])
        s["act"][sh] = part if slot == 0 else s["act"][sh] + part

    zs1 = z_step(1)
    ys = [y_first(0)]
    up(0, 0)

    tok2 = ring_forward(s["tok"], tok1[0])
    cot1 = ring_start(s["cot"])
    for cp in hz_cp:
        cp.wait_recv()
    s["hy"][0] = sum(s["hz"][i] for i in range(NZ))
    hy_cp = [send(s["hy"].at[0], s["hy"].at[r], yr[r]) for r in range(1, NY)]
    tokc0.wait_recv()
    up(1, 0)
    z_wait(zs1)
    zs2 = z_step(2)
    ys.append(y_first(1))

    wait_both(tok1[1])
    tokc = [to_core(s["tok"], i) for i in (1, 3)]
    up(0, 1)
    up(0, 3)
    s["pb"][0] = (dot_nt(one_hot(pool_mask(E, E * PATCH)), patches[...]) * (1.0 / PATCH)).astype(bf16)
    wait_both(tokc)
    up(1, 1)
    up(1, 3)

    wait_both(tok2)
    tokc2 = to_core(s["tok"], 2)
    up(0, 2)
    z_wait(zs2)
    zs3 = z_step(3)
    ys.append(y_first(2))
    tokc2.wait_recv()
    up(1, 2)

    for sh in range(2):

        def act_step(i, carry):
            rows = pl.ds(pl.multiple_of(i * 32, 32), 32)
            v = s["pre"][sh, rows, :]
            cumul = 0.5 * (1.0 + lax.erf(v * 0.7071067811865476))
            density = jnp.exp(-0.5 * v * v) * 0.3989422804014327
            s["hid"][pl.ds(pl.multiple_of(sh * R + i * 32, 32), 32), :] = (v * cumul).astype(bf16)
            s["pre"][sh, rows, :] = cumul + v * density
            return carry

        lax.fori_loop(0, R // 32, act_step, 0)

    cot2 = ring_forward(s["cot"], cot1[0])
    pb_cp = [send(s["pb"].at[0], s["pb"].at[r], xr[r]) for r in range(1, NX)]

    pooled_h = dot(one_hot(pool_mask(2 * K, 2 * R)), s["hid"][...]) * (1.0 / PATCH)
    pooled_h = pooled_h.astype(bf16)
    for slot in range(NX):
        m = dot_nt(pooled_h, s["wdt"][xblock(slot), :])
        s["mb"][0, slot] = m[0:K]
        s["mb"][1, slot] = m[K : 2 * K]
    m_c = send(s["mb"].at[1], s["mr"], sib)

    back(0, 0)
    cotc0.wait_recv()
    back(1, 0)
    z_wait(zs3)
    zs4 = z_step(4)
    ys.append(y_first(3))

    for cp in hy_cp:
        cp.wait_recv()
    counts = sum(s["hy"][i][0:1, :] for i in range(NY))
    lane_r = iota((R, 128), 1).astype(f32)
    weight = []
    for sh in range(2):
        drow = spread(s["dst"][sh, 0:1, 0:K])
        weight.append(1.0 / jnp.sum(jnp.where(lane_r == drow, counts, 0.0), axis=1, keepdims=True))

    wait_both(cot1[1])
    cotc = [to_core(s["cot"], i) for i in (1, 3)]
    back(0, 1)
    back(0, 3)

    gi, gj = iota((G, DP), 0), iota((G, DP), 1)
    base = 22 * lax.div(gi, 24)
    inner = lax.rem(gi, 24)
    place = one_hot((inner < 22) & (gj == base + inner))
    for slot in range(NX):
        for sh in range(2):
            s["tokt"][slot, :, sh * R : (sh + 1) * R] = dot(place, s["tok"][sh, slot]).astype(bf16)

    m_c.wait_recv()
    for slot in range(NX):
        s["mx"][slot] = s["mb"][0, slot] + s["mr"][slot]
    mx_cp = [send(s["mx"].at[NX - r], s["mxr"].at[r], xr[r]) for r in range(1, NX)]

    wait_both(cotc)
    back(1, 1)
    back(1, 3)

    ys2 = []
    for g in (0, 1):
        wait_both(ys[g])
        ys2.append(send(yg(1, g), yg(2, g), yp))
    wait_both(ys[2])
    ys2.append(send(yg(3, 2), yg(2, 2), ym))

    wait_both(cot2)
    cotc2 = to_core(s["cot"], 2)
    back(0, 2)
    z_wait(zs4)
    ys.append(y_first(4))
    cotc2.wait_recv()
    back(1, 2)
    for sh in range(2):
        s["gpre"][sh * R : (sh + 1) * R, :] = (s["act"][sh] * weight[sh] * s["pre"][sh]).astype(bf16)

    def slot_of(delta):
        return lax.rem(x + 2 * NY - y - delta, NX)

    def zrows(zeta):
        return pl.ds(pl.multiple_of(lax.rem(z + zeta, NZ) * CH, 16), CH)

    for delta in range(NY):
        s["gb"][delta] = dot(s["tokt"][slot_of(delta)], s["gpre"][:, CA:FH])

    b_cp = {}

    def b_send(k, delta, up_z):
        out, got = (s["sbp"], s["rbp"]) if up_z else (s["sbm"], s["rbm"])
        value = s["gb"][delta, zrows(4 - k if up_z else 4 + k), :]
        first = 0 if (delta < 2) == up_z else 1
        if k > first:
            b_cp[up_z, k - 1, delta].wait_recv()
            value = value + got[k - 1, delta].astype(f32)
        out[k, delta] = value.astype(bf16)
        b_cp[up_z, k, delta] = send(out.at[k, delta], got.at[k, delta], zp if up_z else zm)

    def b_step(t):
        for i in (0, 1):
            b_send(t - 1, i, True)
            b_send(t - 1, 2 + i, False)
        if t < 4:
            for i in (0, 1):
                b_send(t, 2 + i, True)
                b_send(t, i, False)

    b_step(1)

    def ga(delta):
        s["ga"][delta] = dot(s["tokt"][slot_of(delta)], s["gpre"][:, 0:CA])

    ga(2)
    hg = G // 2
    s["sap"][0, 0:hg, :] = s["ga"][2, 0:hg, :].astype(bf16)
    s["sam"][0, hg:G, :] = s["ga"][2, hg:G, :].astype(bf16)
    as1 = (
        send(s["sap"].at[0, pl.ds(0, hg)], s["rap"].at[0, pl.ds(0, hg)], yp),
        send(s["sam"].at[0, pl.ds(hg, hg)], s["ram"].at[0, pl.ds(hg, hg)], ym),
    )
    ga(1)
    s["sap"][1, hg:G, :] = s["ga"][1, hg:G, :].astype(bf16)
    as2 = [send(s["sap"].at[1, pl.ds(hg, hg)], s["rap"].at[1, pl.ds(hg, hg)], yp)]
    ga(3)
    s["sam"][1, 0:hg, :] = s["ga"][3, 0:hg, :].astype(bf16)
    as2.append(send(s["sam"].at[1, pl.ds(0, hg)], s["ram"].at[1, pl.ds(0, hg)], ym))
    ga(0)

    txt_c = [send(s["txt"].at[0], s["txt"].at[NY], sib)]
    wait_both(ys[3])
    ys2.append(send(yg(3, 3), yg(2, 3), ym))
    wait_both(ys[4])
    ys2.append(send(yg(1, 4), yg(2, 4), yp))
    txt_c += [send(s["txt"].at[i], s["txt"].at[NY + i], sib) for i in (1, 3)]

    for cp in mx_cp:
        cp.wait_recv()
    tok_mean = dot_nt(one_hot(pool_mask(K, R)), s["tok"][0, 0]) * (1.0 / PATCH)
    mixed = s["mx"][0] + s["mxr"][1] + s["mxr"][2] + s["mxr"][3]
    s["lpb"][0] = (tok_mean + mixed).astype(bf16)
    lp_cp = [send(s["lpb"].at[0], s["lpb"].at[r], xr[r]) for r in range(1, NX)]

    b_step(2)

    loads[2].wait()
    for cp in pb_cp:
        cp.wait_recv()
    emb = sum(dot(s["pb"][slot], s["proj"][xblock(slot), :]) for slot in range(NX))
    s["eb"][0] = emb.astype(bf16)
    eb_cp = [send(s["eb"].at[0], s["eb"].at[r], xr[r]) for r in range(1, NX)]

    wait_both(as1)
    s["sap"][1, 0:hg, :] = (s["ga"][1, 0:hg, :] + s["rap"][0, 0:hg, :].astype(f32)).astype(bf16)
    as2.append(send(s["sap"].at[1, pl.ds(0, hg)], s["rap"].at[1, pl.ds(0, hg)], yp))
    s["sam"][1, hg:G, :] = (s["ga"][3, hg:G, :] + s["ram"][0, hg:G, :].astype(f32)).astype(bf16)
    as2.append(send(s["sam"].at[1, pl.ds(hg, hg)], s["ram"].at[1, pl.ds(hg, hg)], ym))

    b_step(3)

    for cp in lp_cp:
        cp.wait_recv()
    emb = sum(dot(s["lpb"][slot], s["proj"][xblock(slot), :]) for slot in range(NX))
    s["leb"][0] = emb.astype(bf16)
    le_cp = [send(s["leb"].at[0], s["leb"].at[r], xr[r]) for r in range(1, NX)]

    def normalise(blocks, out):
        v = [blocks[slot].astype(f32) for slot in range(NX)]
        inv = lax.rsqrt(sum(jnp.sum(e * e, axis=1, keepdims=True) for e in v) + eps)
        for slot in range(NX):
            out[:, slot * EP : (slot + 1) * EP] = (v[slot] * inv).astype(bf16)

    def exp_total(hat):
        n = hat.shape[0]

        def step(i, acc):
            return acc + jnp.exp(logit_scale * dot_nt(hat[...], s["txt"][i]))

        acc = lax.fori_loop(0, 2 * NY, step, jnp.zeros((n, NZ * TB), f32))
        return jnp.sum(acc, axis=1, keepdims=True)

    def own_product(hat, own_col):
        scores = dot_nt(hat[...], s["txt"][0, 0:TB, :])
        mine = own_col == (iota(scores.shape, 1) + x * TB)
        return jnp.sum(jnp.where(mine, scores, 0.0), axis=1, keepdims=True)

    def share(buf, total, own):
        buf[0] = jnp.zeros((8, 128), f32)
        buf[0, 0:1, :] = to_row(total, 128)
        buf[0, 1:2, :] = to_row(own, 128)
        return [send(buf.at[0], buf.at[r], xr[r]) for r in range(1, NX)]

    def loss_row(buf, cps):
        for cp in cps:
            cp.wait_recv()
        tile = buf[0] + buf[1] + buf[2] + buf[3]
        return jnp.log(tile[0:1, :]) - logit_scale * tile[1:2, :]

    for cp in eb_cp:
        cp.wait_recv()
    normalise(s["eb"], s["ihat"])
    for cp in ys2:
        cp.wait_recv()
    txt_c.append(send(s["txt"].at[2], s["txt"].at[NY + 2], sib))
    for cp in txt_c:
        cp.wait_recv()
    r_cp = share(s["rs"], exp_total(s["ihat"]), own_product(s["ihat"], iota((E, 1), 0)))

    b_step(4)

    for cp in as2:
        cp.wait_recv()
    s["a1"][...] = s["ga"][0] + s["rap"][1].astype(f32) + s["ram"][1].astype(f32)
    az = []
    for r in (4, 3, 5, 2, 6, 1, 7):
        s["sz"][r] = s["a1"][zrows(r), :].astype(bf16)
        az.append(send(s["sz"].at[r], s["rz"].at[r], zr[r]))

    for delta in range(NY):
        b_cp[True, 3, delta].wait_recv()
        b_cp[False, 3, delta].wait_recv()
        s["b1"][delta] = s["gb"][delta, zrows(0), :] + s["rbp"][3, delta].astype(f32) + s["rbm"][3, delta].astype(f32)
    by = []
    for r in (2, 1, 3):
        s["sy"][r] = s["b1"][r].astype(bf16)
        by.append(send(s["sy"].at[r], s["ry"].at[r], yr[r]))

    for cp in le_cp:
        cp.wait_recv()
    normalise(s["leb"], s["lhat"])
    kcol = to_col(kf, K)
    l_cp = share(s["ls"], exp_total(s["lhat"]), own_product(s["lhat"], kcol.astype(jnp.int32)))

    ref_row = loss_row(s["rs"], r_cp)
    loss_out[...] = jnp.zeros((8, 2 * E), f32)
    loss_out[0:1, 0:E] = ref_row
    learn_row = loss_row(s["ls"], l_cp)
    picked = jnp.sum(jnp.where(iota((K, E), 1).astype(f32) == kcol, ref_row, 0.0), axis=1, keepdims=True)
    loss_out[0:1, E : 2 * E] = learn_row - to_row(picked, E)

    other = pl.ds(pl.multiple_of((1 - c) * (CH // 2), 8), CH // 2)
    own = pl.ds(pl.multiple_of(c * (CH // 2), 8), CH // 2)
    for cp in by:
        cp.wait_recv()
    s["res"][:, CA:FH] = s["b1"][0] + sum(s["ry"][r].astype(f32) for r in range(1, NY))
    fin = [send(s["res"].at[other, pl.ds(CA, FH - CA)], s["fin"].at[:, pl.ds(CA, FH - CA)], sib)]
    for cp in az:
        cp.wait_recv()
    s["res"][:, 0:CA] = s["a1"][zrows(0), :] + sum(s["rz"][r].astype(f32) for r in range(1, NZ))
    fin.append(send(s["res"].at[other, pl.ds(0, CA)], s["fin"].at[:, pl.ds(0, CA)], sib))
    mine = s["res"][own, :]
    wait_both(fin)
    theirs = s["fin"][...]
    grad_out[:, 0:FH] = jnp.where(c == 0, mine, theirs)
    grad_out[:, FH : 2 * FH] = jnp.where(c == 0, theirs, mine)

    for cp in copies:
        cp.wait_send()


def results(losses, grad, ref_out, learn_out, grad_out):
    ref_out[...] = losses[0:1, 0:E]
    learn_out[...] = losses[0:1, E : E + K]
    grad_out[...] = grad[0:22, :]


def per_device(patches, text, ref_proj, w_up, w_down, kept_index, dest, cotan):
    vmem = pl.BlockSpec(memory_space=pltpu.VMEM)
    hbm = pl.BlockSpec(memory_space=pl.ANY)
    scratch = [pltpu.VMEM(shape, dtype) for shape, dtype in SCRATCH.values()]
    scratch += [
        pltpu.SemaphoreType.DMA((N_COPIES,)),
        pltpu.SemaphoreType.DMA((N_COPIES,)),
        pltpu.SemaphoreType.DMA((N_LOCAL,)),
    ]
    losses, grad = pl.pallas_call(
        kernel,
        out_shape=(jax.ShapeDtypeStruct((8, 2 * E), f32), jax.ShapeDtypeStruct((CH // 2, 2 * FH), f32)),
        in_specs=[vmem] * 5 + [hbm] * 3,
        out_specs=(vmem, vmem),
        scratch_shapes=scratch,
        compiler_params=pltpu.CompilerParams(
            collective_id=0, has_side_effects=True, vmem_limit_bytes=56 * 1024 * 1024
        ),
        name="contrastive_step",
    )(patches.T, text, cotan.T, kept_index.reshape(1, K), dest.reshape(1, K), ref_proj, w_up, w_down)
    ref_loss, learnability, grad_up = pl.pallas_call(
        results,
        out_shape=(
            jax.ShapeDtypeStruct((1, E), f32),
            jax.ShapeDtypeStruct((1, K), f32),
            jax.ShapeDtypeStruct((22, 2 * FH), f32),
        ),
        in_specs=[vmem] * 2,
        out_specs=(vmem,) * 3,
        name="results",
    )(losses, grad)
    return (ref_loss.reshape(E), learnability.reshape(K), grad_up)


def solution(mesh):
    in_specs = (
        P("sel", "mdl"),
        P("sel", "mdl"),
        P(None, "mdl"),
        P(None, "mdl"),
        P("mdl", None),
        P("sel"),
        P("sel"),
        P("sel", "mdl"),
    )
    out_specs = (P("sel"), P("sel"), P("sel", "mdl"))
    return jax.shard_map(
        per_device, mesh=mesh, in_specs=in_specs, out_specs=out_specs, check_vma=False
    )
```

```python
import jax
import jax.numpy as jnp
from jax import lax
from jax.experimental import pallas as pl
from jax.experimental.pallas import tpu as pltpu
from jax.sharding import PartitionSpec as P

logit_scale = 64.0
eps = 1e-06
MESH = pl.DeviceIdType.MESH
f32 = jnp.float32
bf16 = jnp.bfloat16

NX, NY, NZ, NC = 4, 4, 8, 2
D, DP = 1408, 352
FH = 768
EMB, EP = 1024, 256
PATCH, E, K = 6, 128, 64
R = K * PATCH
G = 384
CH = 48
CA = 384
TB = E // NX

POS = {0: 0, 1: 1, 7: 2, 2: 3, 6: 4, 3: 5, 5: 6, 4: 7}
GROUPS = [(0, 1), (1, 2), (3, 2), (5, 2), (7, 1)]

N_COPIES = 150
N_LOCAL = 5


def dot(a, b):
    return lax.dot_general(a, b, (((1,), (0,)), ((), ())), preferred_element_type=f32)


def dot_tn(a, b):
    return lax.dot_general(a, b, (((0,), (0,)), ((), ())), preferred_element_type=f32)


def dot_nt(a, b):
    return lax.dot_general(a, b, (((1,), (1,)), ((), ())), preferred_element_type=f32)


def iota(shape, axis):
    return lax.broadcasted_iota(jnp.int32, shape, axis)


def one_hot(mask):
    return jnp.where(mask, 1.0, 0.0).astype(bf16)


def pool_mask(n_out, n_in):
    first = PATCH * iota((n_out, n_in), 0)
    col = iota((n_out, n_in), 1)
    return (col >= first) & (col < first + PATCH)


def spread(row):
    first = PATCH * iota((R, K), 1)
    line = iota((R, K), 0)
    return jnp.sum(jnp.where((line >= first) & (line < first + PATCH), row, 0.0), axis=1, keepdims=True)


def to_row(col, lanes):
    n = col.shape[0]
    return jnp.sum(jnp.where(iota((n, lanes), 0) == iota((n, lanes), 1), col, 0.0), axis=0, keepdims=True)


def to_col(row, n):
    lanes = row.shape[1]
    return jnp.sum(jnp.where(iota((n, lanes), 0) == iota((n, lanes), 1), row, 0.0), axis=1, keepdims=True)


SCRATCH = dict(
    pat=((DP, E * PATCH), bf16),
    proj=((D, EP), bf16),
    wup=((D, FH), bf16),
    wdn=((FH, D), bf16),
    wdt=((D, FH), bf16),
    tok=((2, NX, DP, R), bf16),
    cot=((2, NX, DP, R), bf16),
    pre=((2, R, FH), f32),
    act=((2, R, FH), f32),
    hid=((2 * R, FH), bf16),
    tokt=((NX, G, 2 * R), bf16),
    gpre=((2 * R, FH), bf16),
    tx=((NX, TB, EP), bf16),
    txt=((2 * NY, NZ * TB, EMB), bf16),
    dst=((2, 8, 128), f32),
    hz=((NZ, 8, 128), f32),
    hy=((NY, 8, 128), f32),
    mb=((2, NX, K, DP), f32),
    mr=((NX, K, DP), f32),
    mx=((NX, K, DP), bf16),
    mxr=((NX, K, DP), bf16),
    lpb=((NX, K, DP), bf16),
    leb=((NX, K, EP), bf16),
    lhat=((K, EMB), bf16),
    pb=((NX, E, DP), bf16),
    eb=((NX, E, EP), bf16),
    ihat=((E, EMB), bf16),
    rs=((NX, 8, 128), f32),
    ls=((NX, 8, 128), f32),
    ga=((NY, G, CA), f32),
    gb=((NY, G, FH - CA), f32),
    a1=((G, CA), f32),
    b1=((NY, CH, FH - CA), f32),
    sbp=((4, NY, CH, FH - CA), bf16),
    sbm=((4, NY, CH, FH - CA), bf16),
    rbp=((4, NY, CH, FH - CA), bf16),
    rbm=((4, NY, CH, FH - CA), bf16),
    sap=((2, G, CA), bf16),
    sam=((2, G, CA), bf16),
    rap=((2, G, CA), bf16),
    ram=((2, G, CA), bf16),
    sz=((NZ, CH, CA), bf16),
    rz=((NZ, CH, CA), bf16),
    sy=((NY, CH, FH - CA), bf16),
    ry=((NY, CH, FH - CA), bf16),
    res=((CH, FH), f32),
    fin=((CH // 2, FH), f32),
)


def kernel(patches_hbm, text, cotan_hbm, kidx, dest, proj_hbm, wup_hbm, wdn_hbm, loss_out, grad_out, *scratch):
    names = list(SCRATCH)
    s = dict(zip(names, scratch[: len(names)]))
    send_sem, recv_sem, local_sem = scratch[len(names) :]

    x = lax.axis_index("mdl")
    sel = lax.axis_index("sel")
    c = lax.rem(sel, NC)
    z = lax.rem(lax.div(sel, NC), NZ)
    y = lax.div(sel, NC * NZ)

    def dev(dx=0, dy=0, dz=0, dc=0):
        yy = lax.rem(y + dy, NY)
        zz = lax.rem(z + dz, NZ)
        cc = lax.rem(c + dc, NC)
        return {"sel": (yy * NZ + zz) * NC + cc, "mdl": lax.rem(x + dx, NX)}

    sib = dev(dc=1)
    xr = [None] + [dev(dx=r) for r in range(1, NX)]
    yr = [None] + [dev(dy=r) for r in range(1, NY)]
    zr = [None] + [dev(dz=r) for r in range(1, NZ)]
    yp, ym, zp, zm = yr[1], yr[NY - 1], zr[1], zr[NZ - 1]
    partners = [sib] + xr[1:] + yr[1:] + zr[1:]

    copies = []

    def send(src, dst, device):
        i = len(copies)
        copy = pltpu.make_async_remote_copy(
            src_ref=src,
            dst_ref=dst,
            send_sem=send_sem.at[i],
            recv_sem=recv_sem.at[i],
            device_id=device,
            device_id_type=MESH,
        )
        copy.start()
        copies.append(copy)
        return copy

    def xblock(slot):
        return pl.ds(pl.multiple_of(lax.rem(x + NX - slot, NX) * DP, 32), DP)

    patches = s["pat"]
    rows_in = [
        pltpu.make_async_copy(patches_hbm, patches, local_sem.at[3]),
        pltpu.make_async_copy(cotan_hbm, s["cot"].at[0, 0], local_sem.at[4]),
    ]
    for load in rows_in:
        load.start()
    barrier = pltpu.get_barrier_semaphore()
    for p in partners:
        pl.semaphore_signal(barrier, inc=1, device_id=p, device_id_type=MESH)
    half = pl.multiple_of(c * FH, FH)
    loads = [
        pltpu.make_async_copy(wdn_hbm.at[pl.ds(half, FH), :], s["wdn"], local_sem.at[0]),
        pltpu.make_async_copy(wup_hbm.at[:, pl.ds(half, FH)], s["wup"], local_sem.at[1]),
        pltpu.make_async_copy(proj_hbm, s["proj"], local_sem.at[2]),
    ]
    for load in loads:
        load.start()

    kf = kidx[...].astype(f32)
    krow = spread(kf)
    line = iota((R, 1), 0).astype(f32)
    entry = spread(iota((1, K), 1).astype(f32))
    want = (PATCH * krow + (line - PATCH * entry)).astype(jnp.int32)
    pick = one_hot(iota((R, E * PATCH), 1) == want)
    s["dst"][0] = jnp.zeros((8, 128), f32)
    s["dst"][0, 0:1, 0:K] = dest[...].astype(f32)
    for load in rows_in:
        load.wait()
    s["tok"][0, 0] = dot_nt(patches[...], pick).astype(bf16)

    pl.semaphore_wait(barrier, len(partners))

    text_cp = [
        send(text.at[pl.ds(pl.multiple_of(lax.rem(x + r, NX) * TB, TB), TB), :], s["tx"].at[r], xr[r])
        for r in range(1, NX)
    ]
    dst_cp = send(s["dst"].at[0], s["dst"].at[1], sib)

    h = DP // 2

    def half_to(buf, src, dst, part, device):
        rows = pl.ds(part * h, h)
        return send(buf.at[0, src, rows, :], buf.at[0, dst, rows, :], device)

    def ring_start(buf):
        first = (half_to(buf, 0, 1, 0, xr[1]), half_to(buf, 0, 3, 1, xr[3]))
        second = (half_to(buf, 0, 1, 1, xr[1]), half_to(buf, 0, 3, 0, xr[3]))
        return first, second

    def ring_forward(buf, first):
        out = []
        first[0].wait_recv()
        out.append(half_to(buf, 1, 2, 0, xr[1]))
        first[1].wait_recv()
        out.append(half_to(buf, 3, 2, 1, xr[3]))
        return out

    def wait_both(pair):
        pair[0].wait_recv()
        pair[1].wait_recv()

    def to_core(buf, slot):
        return send(buf.at[0, slot], buf.at[1, slot], sib)

    tok1 = ring_start(s["tok"])
    tokc0 = to_core(s["tok"], 0)
    cotc0 = to_core(s["cot"], 0)

    dst_cp.wait_recv()
    lane = iota((K, 128), 1).astype(f32)
    chip_hist = jnp.zeros((1, 128), f32)
    for sh in range(2):
        dcol = to_col(s["dst"][sh, 0:1, :], K)
        chip_hist += jnp.sum(jnp.where(lane == dcol, 1.0, 0.0), axis=0, keepdims=True)
    s["hz"][0] = jnp.broadcast_to(chip_hist, (8, 128))
    hz_cp = [send(s["hz"].at[0], s["hz"].at[r], zr[r]) for r in range(1, NZ)]

    loads[0].wait()
    eye = one_hot(iota((128, 128), 0) == iota((128, 128), 1))
    for j in range(D // 128):
        s["wdt"][j * 128 : (j + 1) * 128, :] = dot_nt(eye, s["wdn"][:, j * 128 : (j + 1) * 128]).astype(bf16)
    loads[1].wait()

    s["tx"][0] = text[pl.ds(pl.multiple_of(x * TB, TB), TB), :]
    for cp in text_cp:
        cp.wait_recv()
    tv = [s["tx"][r].astype(f32) for r in range(NX)]
    tsq = sum(jnp.sum(v * v, axis=1, keepdims=True) for v in tv)
    tinv = lax.rsqrt(tsq + eps)
    for r in range(NX):
        s["txt"][0, 0:TB, r * EP : (r + 1) * EP] = (tv[r] * tinv).astype(bf16)

    def tz(slot):
        return s["txt"].at[0, pl.ds(POS[slot] * TB, TB), :]

    def z_step(t):
        out = [send(tz(t - 1), tz(t), zp)]
        if t < NZ // 2:
            out.append(send(tz((NZ - t + 1) % NZ), tz(NZ - t), zm))
        return out

    def z_wait(step):
        for cp in step:
            cp.wait_recv()

    def yg(slot, g):
        first, n = GROUPS[g]
        return s["txt"].at[slot, pl.ds(first * TB, n * TB), :]

    def y_first(g):
        return (send(yg(0, g), yg(1, g), yp), send(yg(0, g), yg(3, g), ym))

    def up(sh, slot):
        part = dot_tn(s["tok"][sh, slot], s["wup"][xblock(slot), :])
        s["pre"][sh] = part if slot == 0 else s["pre"][sh] + part

    def back(sh, slot):
        part = dot_tn(s["cot"][sh, slot], s["wdt"][xblock(slot), :])
        s["act"][sh] = part if slot == 0 else s["act"][sh] + part

    zs1 = z_step(1)
    ys = [y_first(0)]
    up(0, 0)

    tok2 = ring_forward(s["tok"], tok1[0])
    cot1 = ring_start(s["cot"])
    for cp in hz_cp:
        cp.wait_recv()
    s["hy"][0] = sum(s["hz"][i] for i in range(NZ))
    hy_cp = [send(s["hy"].at[0], s["hy"].at[r], yr[r]) for r in range(1, NY)]
    tokc0.wait_recv()
    up(1, 0)
    z_wait(zs1)
    zs2 = z_step(2)
    ys.append(y_first(1))

    wait_both(tok1[1])
    tokc = [to_core(s["tok"], i) for i in (1, 3)]
    up(0, 1)
    up(0, 3)
    s["pb"][0] = (dot_nt(one_hot(pool_mask(E, E * PATCH)), patches[...]) * (1.0 / PATCH)).astype(bf16)
    wait_both(tokc)
    up(1, 1)
    up(1, 3)

    wait_both(tok2)
    tokc2 = to_core(s["tok"], 2)
    up(0, 2)
    z_wait(zs2)
    zs3 = z_step(3)
    ys.append(y_first(2))
    tokc2.wait_recv()
    up(1, 2)

    for sh in range(2):

        def act_step(i, carry):
            rows = pl.ds(pl.multiple_of(i * 32, 32), 32)
            v = s["pre"][sh, rows, :]
            cumul = 0.5 * (1.0 + lax.erf(v * 0.7071067811865476))
            density = jnp.exp(-0.5 * v * v) * 0.3989422804014327
            s["hid"][pl.ds(pl.multiple_of(sh * R + i * 32, 32), 32), :] = (v * cumul).astype(bf16)
            s["pre"][sh, rows, :] = cumul + v * density
            return carry

        lax.fori_loop(0, R // 32, act_step, 0)

    cot2 = ring_forward(s["cot"], cot1[0])
    pb_cp = [send(s["pb"].at[0], s["pb"].at[r], xr[r]) for r in range(1, NX)]

    pooled_h = dot(one_hot(pool_mask(2 * K, 2 * R)), s["hid"][...]) * (1.0 / PATCH)
    pooled_h = pooled_h.astype(bf16)
    for slot in range(NX):
        m = dot_nt(pooled_h, s["wdt"][xblock(slot), :])
        s["mb"][0, slot] = m[0:K]
        s["mb"][1, slot] = m[K : 2 * K]
    m_c = send(s["mb"].at[1], s["mr"], sib)

    back(0, 0)
    cotc0.wait_recv()
    back(1, 0)
    z_wait(zs3)
    zs4 = z_step(4)
    ys.append(y_first(3))

    for cp in hy_cp:
        cp.wait_recv()
    counts = sum(s["hy"][i][0:1, :] for i in range(NY))
    lane_r = iota((R, 128), 1).astype(f32)
    weight = []
    for sh in range(2):
        drow = spread(s["dst"][sh, 0:1, 0:K])
        weight.append(1.0 / jnp.sum(jnp.where(lane_r == drow, counts, 0.0), axis=1, keepdims=True))

    wait_both(cot1[1])
    cotc = [to_core(s["cot"], i) for i in (1, 3)]
    back(0, 1)
    back(0, 3)

    gi, gj = iota((G, DP), 0), iota((G, DP), 1)
    base = 22 * lax.div(gi, 24)
    inner = lax.rem(gi, 24)
    place = one_hot((inner < 22) & (gj == base + inner))
    for slot in range(NX):
        for sh in range(2):
            s["tokt"][slot, :, sh * R : (sh + 1) * R] = dot(place, s["tok"][sh, slot]).astype(bf16)

    m_c.wait_recv()
    for slot in range(NX):
        s["mx"][slot] = (s["mb"][0, slot] + s["mr"][slot]).astype(bf16)
    mx_cp = [send(s["mx"].at[NX - r], s["mxr"].at[r], xr[r]) for r in range(1, NX)]

    wait_both(cotc)
    back(1, 1)
    back(1, 3)

    ys2 = []
    for g in (0, 1):
        wait_both(ys[g])
        ys2.append(send(yg(1, g), yg(2, g), yp))
    wait_both(ys[2])
    ys2.append(send(yg(3, 2), yg(2, 2), ym))

    wait_both(cot2)
    cotc2 = to_core(s["cot"], 2)
    back(0, 2)
    z_wait(zs4)
    ys.append(y_first(4))
    cotc2.wait_recv()
    back(1, 2)
    for sh in range(2):
        s["gpre"][sh * R : (sh + 1) * R, :] = (s["act"][sh] * weight[sh] * s["pre"][sh]).astype(bf16)

    def slot_of(delta):
        return lax.rem(x + 2 * NY - y - delta, NX)

    def zrows(zeta):
        return pl.ds(pl.multiple_of(lax.rem(z + zeta, NZ) * CH, 16), CH)

    for delta in range(NY):
        s["gb"][delta] = dot(s["tokt"][slot_of(delta)], s["gpre"][:, CA:FH])

    b_cp = {}

    def b_send(k, delta, up_z):
        out, got = (s["sbp"], s["rbp"]) if up_z else (s["sbm"], s["rbm"])
        value = s["gb"][delta, zrows(4 - k if up_z else 4 + k), :]
        first = 0 if (delta < 2) == up_z else 1
        if k > first:
            b_cp[up_z, k - 1, delta].wait_recv()
            value = value + got[k - 1, delta].astype(f32)
        out[k, delta] = value.astype(bf16)
        b_cp[up_z, k, delta] = send(out.at[k, delta], got.at[k, delta], zp if up_z else zm)

    def b_step(t):
        for i in (0, 1):
            b_send(t - 1, i, True)
            b_send(t - 1, 2 + i, False)
        if t < 4:
            for i in (0, 1):
                b_send(t, 2 + i, True)
                b_send(t, i, False)

    b_step(1)

    def ga(delta):
        s["ga"][delta] = dot(s["tokt"][slot_of(delta)], s["gpre"][:, 0:CA])

    ga(2)
    hg = G // 2
    s["sap"][0, 0:hg, :] = s["ga"][2, 0:hg, :].astype(bf16)
    s["sam"][0, hg:G, :] = s["ga"][2, hg:G, :].astype(bf16)
    as1 = (
        send(s["sap"].at[0, pl.ds(0, hg)], s["rap"].at[0, pl.ds(0, hg)], yp),
        send(s["sam"].at[0, pl.ds(hg, hg)], s["ram"].at[0, pl.ds(hg, hg)], ym),
    )
    ga(1)
    s["sap"][1, hg:G, :] = s["ga"][1, hg:G, :].astype(bf16)
    as2 = [send(s["sap"].at[1, pl.ds(hg, hg)], s["rap"].at[1, pl.ds(hg, hg)], yp)]
    ga(3)
    s["sam"][1, 0:hg, :] = s["ga"][3, 0:hg, :].astype(bf16)
    as2.append(send(s["sam"].at[1, pl.ds(0, hg)], s["ram"].at[1, pl.ds(0, hg)], ym))
    ga(0)

    b_step(2)

    loads[2].wait()
    for cp in pb_cp:
        cp.wait_recv()
    emb = sum(dot(s["pb"][slot], s["proj"][xblock(slot), :]) for slot in range(NX))
    s["eb"][0] = emb.astype(bf16)
    eb_cp = [send(s["eb"].at[0], s["eb"].at[r], xr[r]) for r in range(1, NX)]

    wait_both(as1)
    s["sap"][1, 0:hg, :] = (s["ga"][1, 0:hg, :] + s["rap"][0, 0:hg, :].astype(f32)).astype(bf16)
    as2.append(send(s["sap"].at[1, pl.ds(0, hg)], s["rap"].at[1, pl.ds(0, hg)], yp))
    s["sam"][1, hg:G, :] = (s["ga"][3, hg:G, :] + s["ram"][0, hg:G, :].astype(f32)).astype(bf16)
    as2.append(send(s["sam"].at[1, pl.ds(hg, hg)], s["ram"].at[1, pl.ds(hg, hg)], ym))

    b_step(3)

    wait_both(ys[3])
    ys2.append(send(yg(3, 3), yg(2, 3), ym))
    wait_both(ys[4])
    ys2.append(send(yg(1, 4), yg(2, 4), yp))
    txt_c = [send(s["txt"].at[i], s["txt"].at[NY + i], sib) for i in (0, 1, 3)]

    for cp in mx_cp:
        cp.wait_recv()
    tok_mean = dot_nt(one_hot(pool_mask(K, R)), s["tok"][0, 0]) * (1.0 / PATCH)
    mixed = s["mb"][0, 0] + s["mr"][0] + sum(s["mxr"][r].astype(f32) for r in range(1, NX))
    s["lpb"][0] = (tok_mean + mixed).astype(bf16)
    lp_cp = [send(s["lpb"].at[0], s["lpb"].at[r], xr[r]) for r in range(1, NX)]

    def normalise(blocks, out):
        v = [blocks[slot].astype(f32) for slot in range(NX)]
        inv = lax.rsqrt(sum(jnp.sum(e * e, axis=1, keepdims=True) for e in v) + eps)
        for slot in range(NX):
            out[:, slot * EP : (slot + 1) * EP] = (v[slot] * inv).astype(bf16)

    def exp_total(hat):
        n = hat.shape[0]

        def step(i, acc):
            return acc + jnp.exp(logit_scale * dot_nt(hat[...], s["txt"][i]))

        acc = lax.fori_loop(0, 2 * NY, step, jnp.zeros((n, NZ * TB), f32))
        return jnp.sum(acc, axis=1, keepdims=True)

    def own_product(hat, own_col):
        scores = dot_nt(hat[...], s["txt"][0, 0:TB, :])
        mine = own_col == (iota(scores.shape, 1) + x * TB)
        return jnp.sum(jnp.where(mine, scores, 0.0), axis=1, keepdims=True)

    def share(buf, total, own):
        buf[0] = jnp.zeros((8, 128), f32)
        buf[0, 0:1, :] = to_row(total, 128)
        buf[0, 1:2, :] = to_row(own, 128)
        return [send(buf.at[0], buf.at[r], xr[r]) for r in range(1, NX)]

    def loss_row(buf, cps):
        for cp in cps:
            cp.wait_recv()
        tile = buf[0] + buf[1] + buf[2] + buf[3]
        return jnp.log(tile[0:1, :]) - logit_scale * tile[1:2, :]

    for cp in eb_cp:
        cp.wait_recv()
    normalise(s["eb"], s["ihat"])

    b_step(4)

    for cp in as2:
        cp.wait_recv()
    s["a1"][...] = s["ga"][0] + s["rap"][1].astype(f32) + s["ram"][1].astype(f32)
    az = []
    for r in (4, 3, 5, 2, 6, 1, 7):
        s["sz"][r] = s["a1"][zrows(r), :].astype(bf16)
        az.append(send(s["sz"].at[r], s["rz"].at[r], zr[r]))

    for cp in lp_cp:
        cp.wait_recv()
    emb = sum(dot(s["lpb"][slot], s["proj"][xblock(slot), :]) for slot in range(NX))
    s["leb"][0] = emb.astype(bf16)
    le_cp = [send(s["leb"].at[0], s["leb"].at[r], xr[r]) for r in range(1, NX)]

    for delta in range(NY):
        b_cp[True, 3, delta].wait_recv()
        b_cp[False, 3, delta].wait_recv()
        s["b1"][delta] = s["gb"][delta, zrows(0), :] + s["rbp"][3, delta].astype(f32) + s["rbm"][3, delta].astype(f32)
    by = []
    for r in (2, 1, 3):
        s["sy"][r] = s["b1"][r].astype(bf16)
        by.append(send(s["sy"].at[r], s["ry"].at[r], yr[r]))

    for cp in ys2:
        cp.wait_recv()
    txt_c.append(send(s["txt"].at[2], s["txt"].at[NY + 2], sib))
    for cp in txt_c:
        cp.wait_recv()
    r_cp = share(s["rs"], exp_total(s["ihat"]), own_product(s["ihat"], iota((E, 1), 0)))

    for cp in le_cp:
        cp.wait_recv()
    normalise(s["leb"], s["lhat"])
    kcol = to_col(kf, K)
    l_cp = share(s["ls"], exp_total(s["lhat"]), own_product(s["lhat"], kcol.astype(jnp.int32)))

    ref_row = loss_row(s["rs"], r_cp)
    loss_out[...] = jnp.zeros((8, 2 * E), f32)
    loss_out[0:1, 0:E] = ref_row
    learn_row = loss_row(s["ls"], l_cp)
    picked = jnp.sum(jnp.where(iota((K, E), 1).astype(f32) == kcol, ref_row, 0.0), axis=1, keepdims=True)
    loss_out[0:1, E : 2 * E] = learn_row - to_row(picked, E)

    other = pl.ds(pl.multiple_of((1 - c) * (CH // 2), 8), CH // 2)
    own = pl.ds(pl.multiple_of(c * (CH // 2), 8), CH // 2)
    for cp in by:
        cp.wait_recv()
    s["res"][:, CA:FH] = s["b1"][0] + sum(s["ry"][r].astype(f32) for r in range(1, NY))
    fin = [send(s["res"].at[other, pl.ds(CA, FH - CA)], s["fin"].at[:, pl.ds(CA, FH - CA)], sib)]
    for cp in az:
        cp.wait_recv()
    s["res"][:, 0:CA] = s["a1"][zrows(0), :] + sum(s["rz"][r].astype(f32) for r in range(1, NZ))
    fin.append(send(s["res"].at[other, pl.ds(0, CA)], s["fin"].at[:, pl.ds(0, CA)], sib))
    mine = s["res"][own, :]
    wait_both(fin)
    theirs = s["fin"][...]
    grad_out[:, 0:FH] = jnp.where(c == 0, mine, theirs)
    grad_out[:, FH : 2 * FH] = jnp.where(c == 0, theirs, mine)

    for cp in copies:
        cp.wait_send()


def results(losses, grad, ref_out, learn_out, grad_out):
    ref_out[...] = losses[0:1, 0:E]
    learn_out[...] = losses[0:1, E : E + K]
    grad_out[...] = grad[0:22, :]


def per_device(patches, text, ref_proj, w_up, w_down, kept_index, dest, cotan):
    vmem = pl.BlockSpec(memory_space=pltpu.VMEM)
    hbm = pl.BlockSpec(memory_space=pl.ANY)
    scratch = [pltpu.VMEM(shape, dtype) for shape, dtype in SCRATCH.values()]
    scratch += [
        pltpu.SemaphoreType.DMA((N_COPIES,)),
        pltpu.SemaphoreType.DMA((N_COPIES,)),
        pltpu.SemaphoreType.DMA((N_LOCAL,)),
    ]
    losses, grad = pl.pallas_call(
        kernel,
        out_shape=(jax.ShapeDtypeStruct((8, 2 * E), f32), jax.ShapeDtypeStruct((CH // 2, 2 * FH), f32)),
        in_specs=[hbm, vmem, hbm, vmem, vmem] + [hbm] * 3,
        out_specs=(vmem, vmem),
        scratch_shapes=scratch,
        compiler_params=pltpu.CompilerParams(
            collective_id=0, has_side_effects=True, vmem_limit_bytes=56 * 1024 * 1024
        ),
        name="contrastive_step",
    )(patches.T, text, cotan.T, kept_index.reshape(1, K), dest.reshape(1, K), ref_proj, w_up, w_down)
    ref_loss, learnability, grad_up = pl.pallas_call(
        results,
        out_shape=(
            jax.ShapeDtypeStruct((1, E), f32),
            jax.ShapeDtypeStruct((1, K), f32),
            jax.ShapeDtypeStruct((22, 2 * FH), f32),
        ),
        in_specs=[vmem] * 2,
        out_specs=(vmem,) * 3,
        name="results",
    )(losses, grad)
    return (ref_loss.reshape(E), learnability.reshape(K), grad_up)


def solution(mesh):
    in_specs = (
        P("sel", "mdl"),
        P("sel", "mdl"),
        P(None, "mdl"),
        P(None, "mdl"),
        P("mdl", None),
        P("sel"),
        P("sel"),
        P("sel", "mdl"),
    )
    out_specs = (P("sel"), P("sel"), P("sel", "mdl"))
    return jax.shard_map(
        per_device, mesh=mesh, in_specs=in_specs, out_specs=out_specs, check_vma=False
    )
```

```python
import jax
import jax.numpy as jnp
from jax import lax
from jax.experimental import pallas as pl
from jax.experimental.pallas import tpu as pltpu
from jax.sharding import PartitionSpec as P

logit_scale = 64.0
eps = 1e-06
MESH = pl.DeviceIdType.MESH
f32 = jnp.float32
bf16 = jnp.bfloat16

NX, NY, NZ, NC = 4, 4, 8, 2
D, DP = 1408, 352
FH = 768
EMB, EP = 1024, 256
PATCH, E, K = 6, 128, 64
R = K * PATCH
G = 384
CH = 48
CA = 384
TB = E // NX

POS = {0: 0, 1: 1, 7: 2, 2: 3, 6: 4, 3: 5, 5: 6, 4: 7}
GROUPS = [(0, 1), (1, 2), (3, 2), (5, 2), (7, 1)]

N_COPIES = 150
N_LOCAL = 5


def dot(a, b):
    return lax.dot_general(a, b, (((1,), (0,)), ((), ())), preferred_element_type=f32)


def dot_tn(a, b):
    return lax.dot_general(a, b, (((0,), (0,)), ((), ())), preferred_element_type=f32)


def dot_nt(a, b):
    return lax.dot_general(a, b, (((1,), (1,)), ((), ())), preferred_element_type=f32)


def iota(shape, axis):
    return lax.broadcasted_iota(jnp.int32, shape, axis)


def one_hot(mask):
    return jnp.where(mask, 1.0, 0.0).astype(bf16)


def pool_mask(n_out, n_in):
    first = PATCH * iota((n_out, n_in), 0)
    col = iota((n_out, n_in), 1)
    return (col >= first) & (col < first + PATCH)


def spread(row):
    first = PATCH * iota((R, K), 1)
    line = iota((R, K), 0)
    return jnp.sum(jnp.where((line >= first) & (line < first + PATCH), row, 0.0), axis=1, keepdims=True)


def to_row(col, lanes):
    n = col.shape[0]
    return jnp.sum(jnp.where(iota((n, lanes), 0) == iota((n, lanes), 1), col, 0.0), axis=0, keepdims=True)


def to_col(row, n):
    lanes = row.shape[1]
    return jnp.sum(jnp.where(iota((n, lanes), 0) == iota((n, lanes), 1), row, 0.0), axis=1, keepdims=True)


SCRATCH = dict(
    pat=((DP, E * PATCH), bf16),
    proj=((D, EP), bf16),
    wup=((D, FH), bf16),
    wdn=((FH, D), bf16),
    wdt=((D, FH), bf16),
    tok=((2, NX, DP, R), bf16),
    cot=((2, NX, DP, R), bf16),
    pre=((2, R, FH), f32),
    act=((2, R, FH), f32),
    hid=((2 * R, FH), bf16),
    tokt=((NX, G, 2 * R), bf16),
    gpre=((2 * R, FH), bf16),
    tx=((NX, TB, EP), bf16),
    txt=((2 * NY, NZ * TB, EMB), bf16),
    dst=((2, 8, 128), f32),
    hz=((NZ, 8, 128), f32),
    hy=((NY, 8, 128), f32),
    mb=((2, NX, K, DP), f32),
    mr=((NX, K, DP), f32),
    mx=((NX, K, DP), bf16),
    mxr=((NX, K, DP), bf16),
    lpb=((NX, K, DP), bf16),
    leb=((NX, K, EP), bf16),
    lhat=((K, EMB), bf16),
    pb=((NX, E, DP), bf16),
    eb=((NX, E, EP), bf16),
    ihat=((E, EMB), bf16),
    rs=((NX, 8, 128), f32),
    ls=((NX, 8, 128), f32),
    ga=((NY, G, CA), f32),
    gb=((NY, G, FH - CA), f32),
    a1=((G, CA), f32),
    b1=((NY, CH, FH - CA), f32),
    sbp=((4, NY, CH, FH - CA), bf16),
    sbm=((4, NY, CH, FH - CA), bf16),
    rbp=((4, NY, CH, FH - CA), bf16),
    rbm=((4, NY, CH, FH - CA), bf16),
    sap=((2, G, CA), bf16),
    sam=((2, G, CA), bf16),
    rap=((2, G, CA), bf16),
    ram=((2, G, CA), bf16),
    sz=((NZ, CH, CA), bf16),
    rz=((NZ, CH, CA), bf16),
    sy=((NY, CH, FH - CA), bf16),
    ry=((NY, CH, FH - CA), bf16),
    res=((CH, FH), f32),
    fin=((CH // 2, FH), f32),
)


def kernel(patches_hbm, text, cotan_hbm, kidx, dest, proj_hbm, wup_hbm, wdn_hbm, loss_out, grad_out, *scratch):
    names = list(SCRATCH)
    s = dict(zip(names, scratch[: len(names)]))
    send_sem, recv_sem, local_sem = scratch[len(names) :]

    x = lax.axis_index("mdl")
    sel = lax.axis_index("sel")
    c = lax.rem(sel, NC)
    z = lax.rem(lax.div(sel, NC), NZ)
    y = lax.div(sel, NC * NZ)

    def dev(dx=0, dy=0, dz=0, dc=0):
        yy = lax.rem(y + dy, NY)
        zz = lax.rem(z + dz, NZ)
        cc = lax.rem(c + dc, NC)
        return {"sel": (yy * NZ + zz) * NC + cc, "mdl": lax.rem(x + dx, NX)}

    sib = dev(dc=1)
    xr = [None] + [dev(dx=r) for r in range(1, NX)]
    yr = [None] + [dev(dy=r) for r in range(1, NY)]
    zr = [None] + [dev(dz=r) for r in range(1, NZ)]
    yp, ym, zp, zm = yr[1], yr[NY - 1], zr[1], zr[NZ - 1]
    partners = [sib] + xr[1:] + yr[1:] + zr[1:]

    copies = []

    def send(src, dst, device):
        i = len(copies)
        copy = pltpu.make_async_remote_copy(
            src_ref=src,
            dst_ref=dst,
            send_sem=send_sem.at[i],
            recv_sem=recv_sem.at[i],
            device_id=device,
            device_id_type=MESH,
        )
        copy.start()
        copies.append(copy)
        return copy

    def xblock(slot):
        return pl.ds(pl.multiple_of(lax.rem(x + NX - slot, NX) * DP, 32), DP)

    patches = s["pat"]
    rows_in = [
        pltpu.make_async_copy(patches_hbm, patches, local_sem.at[3]),
        pltpu.make_async_copy(cotan_hbm, s["cot"].at[0, 0], local_sem.at[4]),
    ]
    for load in rows_in:
        load.start()
    barrier = pltpu.get_barrier_semaphore()
    for p in partners:
        pl.semaphore_signal(barrier, inc=1, device_id=p, device_id_type=MESH)
    half = pl.multiple_of(c * FH, FH)
    loads = [
        pltpu.make_async_copy(wdn_hbm.at[pl.ds(half, FH), :], s["wdn"], local_sem.at[0]),
        pltpu.make_async_copy(wup_hbm.at[:, pl.ds(half, FH)], s["wup"], local_sem.at[1]),
        pltpu.make_async_copy(proj_hbm, s["proj"], local_sem.at[2]),
    ]
    for load in loads:
        load.start()

    kf = kidx[...].astype(f32)
    krow = spread(kf)
    line = iota((R, 1), 0).astype(f32)
    entry = spread(iota((1, K), 1).astype(f32))
    want = (PATCH * krow + (line - PATCH * entry)).astype(jnp.int32)
    pick = one_hot(iota((R, E * PATCH), 1) == want)
    s["dst"][0] = jnp.zeros((8, 128), f32)
    s["dst"][0, 0:1, 0:K] = dest[...].astype(f32)
    for load in rows_in:
        load.wait()
    s["tok"][0, 0] = dot_nt(patches[...], pick).astype(bf16)

    pl.semaphore_wait(barrier, len(partners))

    text_cp = [
        send(text.at[pl.ds(pl.multiple_of(lax.rem(x + r, NX) * TB, TB), TB), :], s["tx"].at[r], xr[r])
        for r in range(1, NX)
    ]
    dst_cp = send(s["dst"].at[0], s["dst"].at[1], sib)

    h = DP // 2

    def half_to(buf, src, dst, part, device):
        rows = pl.ds(part * h, h)
        return send(buf.at[0, src, rows, :], buf.at[0, dst, rows, :], device)

    def ring_start(buf):
        first = (half_to(buf, 0, 1, 0, xr[1]), half_to(buf, 0, 3, 1, xr[3]))
        second = (half_to(buf, 0, 1, 1, xr[1]), half_to(buf, 0, 3, 0, xr[3]))
        return first, second

    def ring_forward(buf, first):
        out = []
        first[0].wait_recv()
        out.append(half_to(buf, 1, 2, 0, xr[1]))
        first[1].wait_recv()
        out.append(half_to(buf, 3, 2, 1, xr[3]))
        return out

    def wait_both(pair):
        pair[0].wait_recv()
        pair[1].wait_recv()

    def to_core(buf, slot):
        return send(buf.at[0, slot], buf.at[1, slot], sib)

    tok1 = ring_start(s["tok"])
    tokc0 = to_core(s["tok"], 0)
    cotc0 = to_core(s["cot"], 0)

    dst_cp.wait_recv()
    lane = iota((K, 128), 1).astype(f32)
    chip_hist = jnp.zeros((1, 128), f32)
    for sh in range(2):
        dcol = to_col(s["dst"][sh, 0:1, :], K)
        chip_hist += jnp.sum(jnp.where(lane == dcol, 1.0, 0.0), axis=0, keepdims=True)
    s["hz"][0] = jnp.broadcast_to(chip_hist, (8, 128))
    hz_cp = [send(s["hz"].at[0], s["hz"].at[r], zr[r]) for r in range(1, NZ)]

    loads[0].wait()
    eye = one_hot(iota((128, 128), 0) == iota((128, 128), 1))
    for j in range(D // 128):
        s["wdt"][j * 128 : (j + 1) * 128, :] = dot_nt(eye, s["wdn"][:, j * 128 : (j + 1) * 128]).astype(bf16)
    loads[1].wait()

    s["tx"][0] = text[pl.ds(pl.multiple_of(x * TB, TB), TB), :]
    for cp in text_cp:
        cp.wait_recv()
    tv = [s["tx"][r].astype(f32) for r in range(NX)]
    tsq = sum(jnp.sum(v * v, axis=1, keepdims=True) for v in tv)
    tinv = lax.rsqrt(tsq + eps)
    for r in range(NX):
        s["txt"][0, 0:TB, r * EP : (r + 1) * EP] = (tv[r] * tinv).astype(bf16)

    def tz(slot):
        return s["txt"].at[0, pl.ds(POS[slot] * TB, TB), :]

    def z_step(t):
        out = [send(tz(t - 1), tz(t), zp)]
        if t < NZ // 2:
            out.append(send(tz((NZ - t + 1) % NZ), tz(NZ - t), zm))
        return out

    def z_wait(step):
        for cp in step:
            cp.wait_recv()

    def yg(slot, g):
        first, n = GROUPS[g]
        return s["txt"].at[slot, pl.ds(first * TB, n * TB), :]

    def y_first(g):
        return (send(yg(0, g), yg(1, g), yp), send(yg(0, g), yg(3, g), ym))

    def up(sh, slot):
        part = dot_tn(s["tok"][sh, slot], s["wup"][xblock(slot), :])
        s["pre"][sh] = part if slot == 0 else s["pre"][sh] + part

    def back(sh, slot):
        part = dot_tn(s["cot"][sh, slot], s["wdt"][xblock(slot), :])
        s["act"][sh] = part if slot == 0 else s["act"][sh] + part

    zs1 = z_step(1)
    ys = [y_first(0)]
    up(0, 0)

    tok2 = ring_forward(s["tok"], tok1[0])
    cot1 = ring_start(s["cot"])
    for cp in hz_cp:
        cp.wait_recv()
    s["hy"][0] = sum(s["hz"][i] for i in range(NZ))
    hy_cp = [send(s["hy"].at[0], s["hy"].at[r], yr[r]) for r in range(1, NY)]
    tokc0.wait_recv()
    up(1, 0)
    z_wait(zs1)
    zs2 = z_step(2)
    ys.append(y_first(1))

    wait_both(tok1[1])
    tokc = [to_core(s["tok"], i) for i in (1, 3)]
    up(0, 1)
    up(0, 3)
    s["pb"][0] = (dot_nt(one_hot(pool_mask(E, E * PATCH)), patches[...]) * (1.0 / PATCH)).astype(bf16)
    wait_both(tokc)
    up(1, 1)
    up(1, 3)

    wait_both(tok2)
    tokc2 = to_core(s["tok"], 2)
    up(0, 2)
    z_wait(zs2)
    zs3 = z_step(3)
    ys.append(y_first(2))
    tokc2.wait_recv()
    up(1, 2)

    for sh in range(2):

        def act_step(i, carry):
            rows = pl.ds(pl.multiple_of(i * 32, 32), 32)
            v = s["pre"][sh, rows, :]
            cumul = 0.5 * (1.0 + lax.erf(v * 0.7071067811865476))
            density = jnp.exp(-0.5 * v * v) * 0.3989422804014327
            s["hid"][pl.ds(pl.multiple_of(sh * R + i * 32, 32), 32), :] = (v * cumul).astype(bf16)
            s["pre"][sh, rows, :] = cumul + v * density
            return carry

        lax.fori_loop(0, R // 32, act_step, 0)

    cot2 = ring_forward(s["cot"], cot1[0])

    pooled_h = dot(one_hot(pool_mask(2 * K, 2 * R)), s["hid"][...]) * (1.0 / PATCH)
    pooled_h = pooled_h.astype(bf16)
    for slot in range(NX):
        m = dot_nt(pooled_h, s["wdt"][xblock(slot), :])
        s["mb"][0, slot] = m[0:K]
        s["mb"][1, slot] = m[K : 2 * K]
    m_c = send(s["mb"].at[1], s["mr"], sib)

    back(0, 0)
    cotc0.wait_recv()
    back(1, 0)
    z_wait(zs3)
    zs4 = z_step(4)
    ys.append(y_first(3))

    for cp in hy_cp:
        cp.wait_recv()
    counts = sum(s["hy"][i][0:1, :] for i in range(NY))
    lane_r = iota((R, 128), 1).astype(f32)
    weight = []
    for sh in range(2):
        drow = spread(s["dst"][sh, 0:1, 0:K])
        weight.append(1.0 / jnp.sum(jnp.where(lane_r == drow, counts, 0.0), axis=1, keepdims=True))

    wait_both(cot1[1])
    cotc = [to_core(s["cot"], i) for i in (1, 3)]
    back(0, 1)
    back(0, 3)

    gi, gj = iota((G, DP), 0), iota((G, DP), 1)
    base = 22 * lax.div(gi, 24)
    inner = lax.rem(gi, 24)
    place = one_hot((inner < 22) & (gj == base + inner))
    for slot in range(NX):
        for sh in range(2):
            s["tokt"][slot, :, sh * R : (sh + 1) * R] = dot(place, s["tok"][sh, slot]).astype(bf16)

    m_c.wait_recv()
    for slot in range(NX):
        s["mx"][slot] = (s["mb"][0, slot] + s["mr"][slot]).astype(bf16)

    wait_both(cotc)
    back(1, 1)
    back(1, 3)

    ys2 = []
    for g in (0, 1):
        wait_both(ys[g])
        ys2.append(send(yg(1, g), yg(2, g), yp))
    wait_both(ys[2])
    ys2.append(send(yg(3, 2), yg(2, 2), ym))

    wait_both(cot2)
    cotc2 = to_core(s["cot"], 2)
    mx_cp = [send(s["mx"].at[NX - r], s["mxr"].at[r], xr[r]) for r in range(1, NX)]
    pb_cp = [send(s["pb"].at[0], s["pb"].at[r], xr[r]) for r in range(1, NX)]
    back(0, 2)
    z_wait(zs4)
    ys.append(y_first(4))
    cotc2.wait_recv()
    back(1, 2)
    for sh in range(2):
        s["gpre"][sh * R : (sh + 1) * R, :] = (s["act"][sh] * weight[sh] * s["pre"][sh]).astype(bf16)

    def slot_of(delta):
        return lax.rem(x + 2 * NY - y - delta, NX)

    def zrows(zeta):
        return pl.ds(pl.multiple_of(lax.rem(z + zeta, NZ) * CH, 16), CH)

    for delta in range(NY):
        s["gb"][delta] = dot(s["tokt"][slot_of(delta)], s["gpre"][:, CA:FH])

    b_cp = {}

    def b_send(k, delta, up_z):
        out, got = (s["sbp"], s["rbp"]) if up_z else (s["sbm"], s["rbm"])
        value = s["gb"][delta, zrows(4 - k if up_z else 4 + k), :]
        first = 0 if (delta < 2) == up_z else 1
        if k > first:
            b_cp[up_z, k - 1, delta].wait_recv()
            value = value + got[k - 1, delta].astype(f32)
        out[k, delta] = value.astype(bf16)
        b_cp[up_z, k, delta] = send(out.at[k, delta], got.at[k, delta], zp if up_z else zm)

    def b_step(t):
        for i in (0, 1):
            b_send(t - 1, i, True)
            b_send(t - 1, 2 + i, False)
        if t < 4:
            for i in (0, 1):
                b_send(t, 2 + i, True)
                b_send(t, i, False)

    b_step(1)

    def ga(delta):
        s["ga"][delta] = dot(s["tokt"][slot_of(delta)], s["gpre"][:, 0:CA])

    ga(2)
    hg = G // 2
    s["sap"][0, 0:hg, :] = s["ga"][2, 0:hg, :].astype(bf16)
    s["sam"][0, hg:G, :] = s["ga"][2, hg:G, :].astype(bf16)
    as1 = (
        send(s["sap"].at[0, pl.ds(0, hg)], s["rap"].at[0, pl.ds(0, hg)], yp),
        send(s["sam"].at[0, pl.ds(hg, hg)], s["ram"].at[0, pl.ds(hg, hg)], ym),
    )
    ga(1)
    s["sap"][1, hg:G, :] = s["ga"][1, hg:G, :].astype(bf16)
    as2 = [send(s["sap"].at[1, pl.ds(hg, hg)], s["rap"].at[1, pl.ds(hg, hg)], yp)]
    ga(3)
    s["sam"][1, 0:hg, :] = s["ga"][3, 0:hg, :].astype(bf16)
    as2.append(send(s["sam"].at[1, pl.ds(0, hg)], s["ram"].at[1, pl.ds(0, hg)], ym))
    ga(0)

    b_step(2)

    loads[2].wait()
    for cp in pb_cp:
        cp.wait_recv()
    emb = sum(dot(s["pb"][slot], s["proj"][xblock(slot), :]) for slot in range(NX))
    s["eb"][0] = emb.astype(bf16)
    eb_cp = [send(s["eb"].at[0], s["eb"].at[r], xr[r]) for r in range(1, NX)]

    wait_both(as1)
    s["sap"][1, 0:hg, :] = (s["ga"][1, 0:hg, :] + s["rap"][0, 0:hg, :].astype(f32)).astype(bf16)
    as2.append(send(s["sap"].at[1, pl.ds(0, hg)], s["rap"].at[1, pl.ds(0, hg)], yp))
    s["sam"][1, hg:G, :] = (s["ga"][3, hg:G, :] + s["ram"][0, hg:G, :].astype(f32)).astype(bf16)
    as2.append(send(s["sam"].at[1, pl.ds(hg, hg)], s["ram"].at[1, pl.ds(hg, hg)], ym))

    b_step(3)

    wait_both(ys[3])
    ys2.append(send(yg(3, 3), yg(2, 3), ym))
    wait_both(ys[4])
    ys2.append(send(yg(1, 4), yg(2, 4), yp))
    txt_c = [send(s["txt"].at[i], s["txt"].at[NY + i], sib) for i in (0, 1, 3)]

    for cp in mx_cp:
        cp.wait_recv()
    tok_mean = dot_nt(one_hot(pool_mask(K, R)), s["tok"][0, 0]) * (1.0 / PATCH)
    mixed = s["mb"][0, 0] + s["mr"][0] + sum(s["mxr"][r].astype(f32) for r in range(1, NX))
    s["lpb"][0] = (tok_mean + mixed).astype(bf16)
    lp_cp = [send(s["lpb"].at[0], s["lpb"].at[r], xr[r]) for r in range(1, NX)]

    def normalise(blocks, out):
        v = [blocks[slot].astype(f32) for slot in range(NX)]
        inv = lax.rsqrt(sum(jnp.sum(e * e, axis=1, keepdims=True) for e in v) + eps)
        for slot in range(NX):
            out[:, slot * EP : (slot + 1) * EP] = (v[slot] * inv).astype(bf16)

    def exp_total(hat):
        n = hat.shape[0]

        def step(i, acc):
            return acc + jnp.exp(logit_scale * dot_nt(hat[...], s["txt"][i]))

        acc = lax.fori_loop(0, 2 * NY, step, jnp.zeros((n, NZ * TB), f32))
        return jnp.sum(acc, axis=1, keepdims=True)

    def own_product(hat, own_col):
        scores = dot_nt(hat[...], s["txt"][0, 0:TB, :])
        mine = own_col == (iota(scores.shape, 1) + x * TB)
        return jnp.sum(jnp.where(mine, scores, 0.0), axis=1, keepdims=True)

    def share(buf, total, own):
        buf[0] = jnp.zeros((8, 128), f32)
        buf[0, 0:1, :] = to_row(total, 128)
        buf[0, 1:2, :] = to_row(own, 128)
        return [send(buf.at[0], buf.at[r], xr[r]) for r in range(1, NX)]

    def loss_row(buf, cps):
        for cp in cps:
            cp.wait_recv()
        tile = buf[0] + buf[1] + buf[2] + buf[3]
        return jnp.log(tile[0:1, :]) - logit_scale * tile[1:2, :]

    for cp in eb_cp:
        cp.wait_recv()
    normalise(s["eb"], s["ihat"])

    b_step(4)

    for cp in as2:
        cp.wait_recv()
    s["a1"][...] = s["ga"][0] + s["rap"][1].astype(f32) + s["ram"][1].astype(f32)
    az = []
    for r in (4, 3, 5, 2, 6, 1, 7):
        s["sz"][r] = s["a1"][zrows(r), :].astype(bf16)
        az.append(send(s["sz"].at[r], s["rz"].at[r], zr[r]))

    for cp in lp_cp:
        cp.wait_recv()
    emb = sum(dot(s["lpb"][slot], s["proj"][xblock(slot), :]) for slot in range(NX))
    s["leb"][0] = emb.astype(bf16)
    le_cp = [send(s["leb"].at[0], s["leb"].at[r], xr[r]) for r in range(1, NX)]

    for delta in range(NY):
        b_cp[True, 3, delta].wait_recv()
        b_cp[False, 3, delta].wait_recv()
        s["b1"][delta] = s["gb"][delta, zrows(0), :] + s["rbp"][3, delta].astype(f32) + s["rbm"][3, delta].astype(f32)
    by = []
    for r in (2, 1, 3):
        s["sy"][r] = s["b1"][r].astype(bf16)
        by.append(send(s["sy"].at[r], s["ry"].at[r], yr[r]))

    for cp in ys2:
        cp.wait_recv()
    txt_c.append(send(s["txt"].at[2], s["txt"].at[NY + 2], sib))
    for cp in txt_c:
        cp.wait_recv()
    r_cp = share(s["rs"], exp_total(s["ihat"]), own_product(s["ihat"], iota((E, 1), 0)))

    for cp in le_cp:
        cp.wait_recv()
    normalise(s["leb"], s["lhat"])
    kcol = to_col(kf, K)
    l_cp = share(s["ls"], exp_total(s["lhat"]), own_product(s["lhat"], kcol.astype(jnp.int32)))

    ref_row = loss_row(s["rs"], r_cp)
    loss_out[...] = jnp.zeros((8, 2 * E), f32)
    loss_out[0:1, 0:E] = ref_row
    learn_row = loss_row(s["ls"], l_cp)
    picked = jnp.sum(jnp.where(iota((K, E), 1).astype(f32) == kcol, ref_row, 0.0), axis=1, keepdims=True)
    loss_out[0:1, E : 2 * E] = learn_row - to_row(picked, E)

    other = pl.ds(pl.multiple_of((1 - c) * (CH // 2), 8), CH // 2)
    own = pl.ds(pl.multiple_of(c * (CH // 2), 8), CH // 2)
    for cp in by:
        cp.wait_recv()
    s["res"][:, CA:FH] = s["b1"][0] + sum(s["ry"][r].astype(f32) for r in range(1, NY))
    fin = [send(s["res"].at[other, pl.ds(CA, FH - CA)], s["fin"].at[:, pl.ds(CA, FH - CA)], sib)]
    for cp in az:
        cp.wait_recv()
    s["res"][:, 0:CA] = s["a1"][zrows(0), :] + sum(s["rz"][r].astype(f32) for r in range(1, NZ))
    fin.append(send(s["res"].at[other, pl.ds(0, CA)], s["fin"].at[:, pl.ds(0, CA)], sib))
    mine = s["res"][own, :]
    wait_both(fin)
    theirs = s["fin"][...]
    grad_out[:, 0:FH] = jnp.where(c == 0, mine, theirs)
    grad_out[:, FH : 2 * FH] = jnp.where(c == 0, theirs, mine)

    for cp in copies:
        cp.wait_send()


def results(losses, grad, ref_out, learn_out, grad_out):
    ref_out[...] = losses[0:1, 0:E]
    learn_out[...] = losses[0:1, E : E + K]
    grad_out[...] = grad[0:22, :]


def per_device(patches, text, ref_proj, w_up, w_down, kept_index, dest, cotan):
    vmem = pl.BlockSpec(memory_space=pltpu.VMEM)
    hbm = pl.BlockSpec(memory_space=pl.ANY)
    scratch = [pltpu.VMEM(shape, dtype) for shape, dtype in SCRATCH.values()]
    scratch += [
        pltpu.SemaphoreType.DMA((N_COPIES,)),
        pltpu.SemaphoreType.DMA((N_COPIES,)),
        pltpu.SemaphoreType.DMA((N_LOCAL,)),
    ]
    losses, grad = pl.pallas_call(
        kernel,
        out_shape=(jax.ShapeDtypeStruct((8, 2 * E), f32), jax.ShapeDtypeStruct((CH // 2, 2 * FH), f32)),
        in_specs=[hbm, vmem, hbm, vmem, vmem] + [hbm] * 3,
        out_specs=(vmem, vmem),
        scratch_shapes=scratch,
        compiler_params=pltpu.CompilerParams(
            collective_id=0, has_side_effects=True, vmem_limit_bytes=56 * 1024 * 1024
        ),
        name="contrastive_step",
    )(patches.T, text, cotan.T, kept_index.reshape(1, K), dest.reshape(1, K), ref_proj, w_up, w_down)
    ref_loss, learnability, grad_up = pl.pallas_call(
        results,
        out_shape=(
            jax.ShapeDtypeStruct((1, E), f32),
            jax.ShapeDtypeStruct((1, K), f32),
            jax.ShapeDtypeStruct((22, 2 * FH), f32),
        ),
        in_specs=[vmem] * 2,
        out_specs=(vmem,) * 3,
        name="results",
    )(losses, grad)
    return (ref_loss.reshape(E), learnability.reshape(K), grad_up)


def solution(mesh):
    in_specs = (
        P("sel", "mdl"),
        P("sel", "mdl"),
        P(None, "mdl"),
        P(None, "mdl"),
        P("mdl", None),
        P("sel"),
        P("sel"),
        P("sel", "mdl"),
    )
    out_specs = (P("sel"), P("sel"), P("sel", "mdl"))
    return jax.shard_map(
        per_device, mesh=mesh, in_specs=in_specs, out_specs=out_specs, check_vma=False
    )
```
